512 devices in a mesh: dp: 4 (over y_hi), seq: 128 (over y_lo, x, z, core).
Axes of the slice: x: 4, y: 8 (y_hi: 4, y_lo: 2; y = y_hi * 2 + y_lo), z: 8, core: 2. Of those that a mesh axis runs over, the one named last changes fastest.
Arguments:
- queries: bfloat16 [4, 16384, 512], P('dp', 'seq'), may hold values from -6 to 6
- key_rows: bfloat16 [4, 16384, 512], P('dp', 'seq'), may hold values from -6 to 6
- value_rows: bfloat16 [4, 16384, 512], P('dp', 'seq'), may hold values from -6 to 6
- out_grad: bfloat16 [4, 16384, 1024], P('dp', 'seq'), may hold values from -6 to 6
- out_weight: bfloat16 [512, 1024], P('seq'), may hold values from -0.25 to 0.25
- norm_gain: float32 [256], replicated, may hold values from 0.1 to 1.9
Outputs:
- query_grad: bfloat16 [4, 16384, 512], P('dp', 'seq')
- key_grad: bfloat16 [4, 16384, 512], P('dp', 'seq')
- value_grad: bfloat16 [4, 16384, 512], P('dp', 'seq')
- weight_grad: float32 [512, 1024], P('seq')
The draws below stay inside these ranges and needn't reach their ends.
All inputs are finite; a program needn't handle non-finite values.
Results may differ from the reference program's by a relative error of at most 0.025.
Values may be sent and summed in bfloat16 or wider, within the bound.
A program may use at most 64 MiB of HBM per device.

```python
import math
import jax
import jax.numpy as jnp
from jax import lax

D = 1024
DH = 128
SOFT_HEADS = 2
LIN_HEADS = 2
HD = 512
WINDOW = 256
HALF = 128
TOKENS = 16384
PLASMIDS = 4


def drawn_pair(key):
    query_key = jax.random.fold_in(key, 101)
    key_key = jax.random.fold_in(key, 202)
    full_shape = (PLASMIDS, TOKENS, HD)
    query_draw = jax.random.truncated_normal(query_key, -4.0, 4.0, full_shape, jnp.float32)
    key_draw = jax.random.truncated_normal(key_key, -4.0, 4.0, full_shape, jnp.float32)
    return (query_draw, key_draw)


def linear_columns(key):
    lin_shape = (PLASMIDS, TOKENS, LIN_HEADS, DH)
    query_hot = jax.random.bernoulli(jax.random.fold_in(key, 404), 4.0 / DH, lin_shape)
    key_pick = jax.random.randint(jax.random.fold_in(key, 505), (PLASMIDS, TOKENS, LIN_HEADS, 1), 0, DH)
    key_hot = jnp.arange(DH, dtype=jnp.int32) == key_pick
    low_lo, low_hi, high_lo, high_hi = (-6.0, -2.0, 2.0, 6.0)
    boost_lo, boost_hi = (1.5, 3.5)
    value_base = jax.random.truncated_normal(jax.random.fold_in(key, 1010), -5.0, 5.0, lin_shape, jnp.float32)
    query_low = jax.random.uniform(jax.random.fold_in(key, 606), lin_shape, jnp.float32, low_lo, low_hi)
    query_high = jax.random.uniform(jax.random.fold_in(key, 707), lin_shape, jnp.float32, high_lo, high_hi)
    key_low = jax.random.uniform(jax.random.fold_in(key, 808), lin_shape, jnp.float32, low_lo, low_hi)
    key_high = jax.random.uniform(jax.random.fold_in(key, 909), lin_shape, jnp.float32, high_lo, high_hi)
    value_boost = jax.random.uniform(jax.random.fold_in(key, 1111), lin_shape, jnp.float32, boost_lo, boost_hi)
    query_lin = jnp.where(query_hot, query_high, query_low)
    key_lin = jnp.where(key_hot, key_high, key_low)
    value_lin = jnp.where(key_hot, value_boost, value_base)
    flat_shape = (PLASMIDS, TOKENS, LIN_HEADS * DH)
    return (query_lin.reshape(flat_shape), key_lin.reshape(flat_shape), value_lin.reshape(flat_shape))


def draw_queries(key, part):
    soft = SOFT_HEADS * DH
    soft_part = drawn_pair(key)[0][:, :, :soft]
    lin_part = linear_columns(key)[0]
    return jnp.concatenate([soft_part, lin_part], axis=2).astype(jnp.bfloat16)


def draw_key_rows(key, part):
    soft = SOFT_HEADS * DH
    soft_part = drawn_pair(key)[1][:, :, :soft]
    lin_part = linear_columns(key)[1]
    return jnp.concatenate([soft_part, lin_part], axis=2).astype(jnp.bfloat16)


def draw_value_rows(key, part):
    soft = SOFT_HEADS * DH
    soft_shape = (PLASMIDS, TOKENS, soft)
    soft_part = jax.random.truncated_normal(jax.random.fold_in(key, 1212), -6.0, 6.0, soft_shape, jnp.float32)
    lin_part = linear_columns(key)[2]
    return jnp.concatenate([soft_part, lin_part], axis=2).astype(jnp.bfloat16)


def steps_of(rng, dims, split, least, largest):
    def one(dim, blocks):
        draws = jax.random.uniform(jax.random.fold_in(jax.random.fold_in(rng, 6), dim), (blocks,), jnp.float32, least / len(split), largest / len(split))
        return jnp.repeat(jnp.exp(draws), dims[dim] // blocks).reshape((-1,) + (1,) * (len(dims) - dim - 1))

    level = one(*split[0])
    for cut in split[1:]:
        level = level * one(*cut)
    return level


def normal_values(rng, shape, spread, bound, shards=(), held_as=jnp.bfloat16):
    entries = spread * jax.random.normal(rng, shape, jnp.float32)
    if shards:
        entries = entries * steps_of(rng, shape, shards, -0.22, 0.18)
    return jnp.clip(entries, -bound, bound).astype(held_as)


def setup_inputs(seed: int = 0) -> dict:
    seeds = jax.random.split(jax.random.key(seed), 7)
    queries = draw_queries(jax.random.fold_in(seeds[6], 71), 0)
    key_rows = draw_key_rows(jax.random.fold_in(seeds[6], 71), 0)
    value_rows = draw_value_rows(jax.random.fold_in(seeds[6], 71), 0)
    out_grad = normal_values(seeds[3], (PLASMIDS, TOKENS, D), 1.0, 6.0, ((0, 4), (1, 128)))
    out_weight = normal_values(seeds[4], (HD, D), HD ** -0.5, 0.25, ((0, 128),))
    norm_gain = jnp.clip(1.0 + 0.18 * jax.random.normal(seeds[5], (LIN_HEADS * DH,), jnp.float32), 0.1, 1.9)
    return dict(queries=queries, key_rows=key_rows, value_rows=value_rows, out_grad=out_grad, out_weight=out_weight, norm_gain=norm_gain)


norm_eps = 1e-06

def unit_plus(values):
    return jnp.where(values > 0, values + 1.0, jnp.exp(jnp.minimum(values, 0.0)))

def unit_slope(values):
    return jnp.where(values > 0, 1.0, jnp.exp(jnp.minimum(values, 0.0)))

def one_plasmid(query_all, key_all, value_all, grad_out, out_weight, norm_gain):
    soft = SOFT_HEADS * DH
    factor = DH ** (-0.5)
    highest = lax.Precision.HIGHEST
    d_attn = jnp.dot(grad_out, out_weight.T, preferred_element_type=jnp.float32).astype(jnp.bfloat16)
    query_lin = query_all[:, soft:].astype(jnp.float32).reshape(TOKENS, LIN_HEADS, DH)
    key_lin = key_all[:, soft:].astype(jnp.float32).reshape(TOKENS, LIN_HEADS, DH)
    value_lin = value_all[:, soft:].astype(jnp.float32).reshape(TOKENS, LIN_HEADS, DH)
    phi_query = unit_plus(query_lin)
    phi_key = unit_plus(key_lin)
    lin_state = jnp.einsum('jha,jhb->hab', phi_key, value_lin, precision=highest)
    lin_u = jnp.einsum('iha,hab->ihb', phi_query, lin_state, precision=highest)
    lin_r = lax.rsqrt(lax.optimization_barrier(jnp.mean(lin_u * lin_u, axis=2, keepdims=True)) + norm_eps)
    gain_heads = norm_gain.reshape(LIN_HEADS, DH)
    attn_lin = (gain_heads * lin_u * lin_r).astype(jnp.bfloat16)
    lin_grad = gain_heads * d_attn[:, soft:].astype(jnp.float32).reshape(TOKENS, LIN_HEADS, DH)
    grad_u = lin_r * lin_grad - lin_u * lin_r ** 3 * lax.optimization_barrier(jnp.mean(lin_grad * lin_u, axis=2, keepdims=True))
    dstate = jnp.einsum('iha,ihb->hab', phi_query, grad_u, precision=highest)
    dq_lin = jnp.einsum('ihb,hab->iha', grad_u, lin_state, precision=highest) * unit_slope(query_lin)
    dk_lin = jnp.einsum('jhb,hab->jha', value_lin, dstate, precision=highest) * unit_slope(key_lin)
    dv_lin = jnp.einsum('jha,hab->jhb', phi_key, dstate, precision=highest)
    soft_query = query_all[:, :soft]
    soft_key = key_all[:, :soft]
    soft_value = value_all[:, :soft]
    soft_dattn = d_attn[:, :soft]
    span_rows = 3 * HALF
    row_pos = lax.broadcasted_iota(jnp.int32, (HALF, span_rows), 0)
    col_pos = lax.broadcasted_iota(jnp.int32, (HALF, span_rows), 1)
    inside = (col_pos >= row_pos) & (col_pos < row_pos + WINDOW)

    def block_step(totals, block_index):
        key_total, value_total = totals
        first_row = block_index * HALF
        key_index = (first_row - HALF + jnp.arange(span_rows, dtype=jnp.int32)) % TOKENS
        q_block = lax.dynamic_slice_in_dim(soft_query, first_row, HALF, 0).astype(jnp.float32).reshape(HALF, SOFT_HEADS, DH)
        da_block = lax.dynamic_slice_in_dim(soft_dattn, first_row, HALF, 0).astype(jnp.float32).reshape(HALF, SOFT_HEADS, DH)
        k_span = jnp.take(soft_key, key_index, axis=0).astype(jnp.float32).reshape(span_rows, SOFT_HEADS, DH)
        v_span = jnp.take(soft_value, key_index, axis=0).astype(jnp.float32).reshape(span_rows, SOFT_HEADS, DH)
        scores = jnp.einsum('ihd,jhd->hij', q_block, k_span) * factor
        scores = jnp.where(inside, scores, -1e+30)
        row_peak = lax.optimization_barrier(jnp.max(scores, axis=2, keepdims=True))
        exp_terms = jnp.where(inside, jnp.exp(scores - row_peak), 0.0)
        attn_probs = exp_terms / lax.optimization_barrier(jnp.sum(exp_terms, axis=2, keepdims=True))
        probs_low = attn_probs.astype(jnp.bfloat16)
        probs_wide = probs_low.astype(jnp.float32)
        attn_soft = jnp.einsum('hij,jhd->ihd', probs_wide, v_span).astype(jnp.bfloat16)
        dprob = jnp.einsum('ihd,jhd->hij', da_block, v_span)
        row_delta = lax.optimization_barrier(jnp.sum(da_block * attn_soft.astype(jnp.float32), axis=2))
        dscore = (attn_probs * (dprob - row_delta.T[:, :, None])).astype(jnp.bfloat16).astype(jnp.float32)
        dq_soft = jnp.einsum('hij,jhd->ihd', dscore, k_span) * factor
        dk_span = jnp.einsum('hij,ihd->jhd', dscore, q_block) * factor
        dv_span = jnp.einsum('hij,ihd->jhd', probs_wide, da_block)
        key_total = key_total.at[key_index].add(dk_span.reshape(span_rows, soft))
        value_total = value_total.at[key_index].add(dv_span.reshape(span_rows, soft))
        return ((key_total, value_total), (attn_soft.reshape(HALF, soft), dq_soft.reshape(HALF, soft)))
    zeros_init = jnp.zeros((TOKENS, soft), jnp.float32)
    block_ids = jnp.arange(TOKENS // HALF, dtype=jnp.int32)
    (dk_soft, dv_soft), (attn_soft, dq_soft) = lax.scan(block_step, (zeros_init, zeros_init), block_ids)
    attn = jnp.concatenate([attn_soft.reshape(TOKENS, soft), attn_lin.reshape(TOKENS, LIN_HEADS * DH)], axis=1)
    weight_term = jnp.dot(attn.T, grad_out, preferred_element_type=jnp.float32)
    query_grad = jnp.concatenate([dq_soft.reshape(TOKENS, soft), dq_lin.reshape(TOKENS, LIN_HEADS * DH)], axis=1).astype(jnp.bfloat16)
    key_grad = jnp.concatenate([dk_soft, dk_lin.reshape(TOKENS, LIN_HEADS * DH)], axis=1).astype(jnp.bfloat16)
    value_grad = jnp.concatenate([dv_soft, dv_lin.reshape(TOKENS, LIN_HEADS * DH)], axis=1).astype(jnp.bfloat16)
    return (query_grad, key_grad, value_grad, weight_term)

def reference(queries, key_rows, value_rows, out_grad, out_weight, norm_gain):
    query_list = []
    key_list = []
    value_list = []
    weight_sum = jnp.zeros((HD, D), jnp.float32)
    for plasmid in range(PLASMIDS):
        query_grad, key_grad, value_grad, weight_term = one_plasmid(queries[plasmid], key_rows[plasmid], value_rows[plasmid], out_grad[plasmid], out_weight, norm_gain)
        query_list.append(query_grad)
        key_list.append(key_grad)
        value_list.append(value_grad)
        weight_sum = weight_sum + weight_term
    weight_grad = weight_sum * (1.0 / math.sqrt(PLASMIDS * TOKENS))
    return (jnp.stack(query_list), jnp.stack(key_list), jnp.stack(value_list), weight_grad)
```

```python
import math

import jax
import jax.numpy as jnp
from jax import lax
from jax.experimental import pallas as pl
from jax.experimental.pallas import tpu as pltpu
from jax.sharding import PartitionSpec as P

MESH = pl.DeviceIdType.MESH
DH = 128
ROWS = 128
SOFT = 256
N_SEQ = 128
N_DP = 4
norm_eps = 1e-06
BF16 = jnp.bfloat16
F32 = jnp.float32
FAR = (4, 3, 5, 2, 6, 1, 7)


def dot(a, b, a_dim, b_dim):
    return lax.dot_general(a, b, (((a_dim,), (b_dim,)), ((), ())), preferred_element_type=F32)


def parts(x):
    high = x.astype(BF16)
    return high, (x - high.astype(F32)).astype(BF16)


def dot_wide(a, b, a_dim, b_dim):
    if b.dtype == BF16:
        high, low = parts(a)
        return dot(high, b, a_dim, b_dim) + dot(low, b, a_dim, b_dim)
    if a.dtype == BF16:
        high, low = parts(b)
        return dot(a, high, a_dim, b_dim) + dot(a, low, a_dim, b_dim)
    a_high, a_low = parts(a)
    b_high, b_low = parts(b)
    return (
        dot(a_high, b_high, a_dim, b_dim)
        + dot(a_high, b_low, a_dim, b_dim)
        + dot(a_low, b_high, a_dim, b_dim)
    )


def unit_plus(x):
    return jnp.where(x > 0, x + 1.0, jnp.exp(jnp.minimum(x, 0.0)))


def unit_slope(x):
    return jnp.where(x > 0, 1.0, jnp.exp(jnp.minimum(x, 0.0)))


def head(h):
    return slice(h * DH, (h + 1) * DH)


def kernel(
    q_hbm, k_hbm, v_hbm, g_hbm, w_hbm, gain_hbm,
    dq_ref, dk_ref, dv_ref, wg_ref,
    q_ref, k_ref, v_ref, g_ref, w_ref, gain_ref,
    kx, vx, term, term_in, s_one, s_xy, s_z, s_full,
    w_in, w_rows, w_all, g_in, attn_own, attn_in,
    probs, u_keep, wg_out, wg_in, wg_zout, wg_zin, wg_dp, wg_sum, wg_fin,
    back_out, back_in, dkv_keep,
    lsem, ssem, rsem,
):
    dp = lax.axis_index("dp")
    seq = lax.axis_index("seq")
    core = seq % 2
    z = (seq // 2) % 8
    p = seq // 16
    y = p // 4
    other = 1 - core
    partner = seq + 1 - 2 * core
    after = (seq + 1) % N_SEQ
    before = (seq + N_SEQ - 1) % N_SEQ
    factor = DH ** (-0.5)

    loads = [
        pltpu.make_async_copy(src, dst, lsem.at[i])
        for i, (src, dst) in enumerate(
            (
                (k_hbm, k_ref),
                (v_hbm, v_ref),
                (w_hbm, w_ref),
                (q_hbm, q_ref),
                (gain_hbm, gain_ref),
                (g_hbm, g_ref),
            )
        )
    ]
    for load in loads:
        load.start()

    def xy_peer(d):
        return (((p + d) % 8) * 8 + z) * 2 + core

    def z_peer(d):
        return (p * 8 + (z + d) % 8) * 2 + core

    def z_cross(d):
        return (p * 8 + (z + d) % 8) * 2 + other

    y_peer = xy_peer(4)
    y_cross = (((p + 4) % 8) * 8 + z) * 2 + other

    barrier = pltpu.get_barrier_semaphore()
    peers = [((dp + d) % N_DP, seq) for d in (2, 1, 3)]
    peers += [(dp, z_peer(d)) for d in FAR]
    peers += [(dp, z_cross(d)) for d in FAR]
    peers += [(dp, xy_peer(d)) for d in FAR]
    peers += [(dp, partner), (dp, after), (dp, before), (dp, y_cross)]
    for peer in peers:
        pl.semaphore_signal(barrier, inc=1, device_id=peer, device_id_type=MESH)

    used = [0]
    started = []

    def send(src, dst, device, dp_to=None):
        index = used[0]
        used[0] += 1
        copy = pltpu.make_async_remote_copy(
            src_ref=src,
            dst_ref=dst,
            send_sem=ssem.at[index],
            recv_sem=rsem.at[index],
            device_id=(dp if dp_to is None else dp_to, device),
            device_id_type=MESH,
        )
        copy.start()
        started.append(copy)
        return copy

    def arrived(copies):
        for copy in copies:
            copy.wait_recv()

    class Total:
        def __init__(self, slot, terms):
            self.i = slot
            for h in range(2):
                term[slot, h] = terms[h]

        def start(self):
            i = self.i
            self.c = [send(term.at[i, other], term_in.at[i], partner)]

        def xy(self):
            i = self.i
            arrived(self.c)
            s_one[i] = (term[i, core] + term_in[i]).reshape(8, 16, DH)
            self.c = [send(s_one.at[i, (p + d) % 8], s_xy.at[i, d], xy_peer(d)) for d in FAR]

        def along_z(self):
            i = self.i
            arrived(self.c)
            total = s_one[i, p]
            for d in range(1, 8):
                total = total + s_xy[i, d]
            s_z[i, z] = total
            self.c = [send(s_z.at[i, z], s_z.at[i, z], z_peer(d)) for d in FAR]

        def spread(self):
            i = self.i
            arrived(self.c)
            total = s_z[i, 0]
            for d in range(1, 8):
                total = total + s_z[i, d]
            s_full[i, core, p] = total
            mine = s_full.at[i, core, p]
            self.c = [send(mine, mine, xy_peer(d)) for d in FAR]

        def swap(self):
            i = self.i
            arrived(self.c)
            mine = s_full.at[i, core]
            self.c = [send(mine, mine, partner)]

        def value(self):
            arrived(self.c)
            return [s_full[self.i, h].reshape(DH, DH) for h in range(2)]

    class Half:
        def __init__(self, half, g_mine, g_other):
            self.s = s = half
            for b in range(4):
                rows = slice(s * SOFT + b * 64, s * SOFT + (b + 1) * 64)
                block = dot(attn_own[:, rows], g_mine, 0, 0) + dot(attn_in[:, rows], g_other, 0, 0)
                block = block.astype(BF16)
                wg_out[s, b] = block[:, 0:256]
                wg_out[s, 4 + b] = block[:, 256:512]

        def xy(self):
            s = self.s
            self.c = [send(wg_out.at[s, (p + d) % 8], wg_in.at[s, d], xy_peer(d)) for d in FAR]

        def along_z(self):
            s = self.s
            arrived(self.c)
            total = wg_out[s, p].astype(F32)
            for d in range(1, 8):
                total = total + wg_in[s, d].astype(F32)
            wg_zout[s] = total.reshape(8, 8, 256)
            self.c = [send(wg_zout.at[s, (z + d) % 8], wg_zin.at[s, d], z_peer(d)) for d in FAR]

        def plasmids(self):
            s = self.s
            arrived(self.c)
            total = wg_zout[s, z]
            for d in range(1, 8):
                total = total + wg_zin[s, d]
            wg_dp[s, dp] = total
            mine = wg_dp.at[s, dp]
            self.c = [send(mine, mine, seq, (dp + d) % N_DP) for d in (2, 1, 3)]

        def value(self):
            s = self.s
            arrived(self.c)
            total = (wg_dp[s, 0] + wg_dp[s, 1]) + (wg_dp[s, 2] + wg_dp[s, 3])
            wg_sum[s] = total * (1.0 / math.sqrt(N_DP * N_SEQ * ROWS))

    loads[0].wait()
    loads[1].wait()
    state_sum = Total(
        0,
        [
            dot_wide(unit_plus(k_ref[:, head(2 + h)].astype(F32)), v_ref[:, head(2 + h)], 0, 0)
            for h in range(2)
        ],
    )
    loads[2].wait()
    w_in[z * 2 + core] = jnp.where(
        core == 0, w_ref[:, 0:512].astype(F32), w_ref[:, 512:1024].astype(F32)
    ).astype(BF16)

    pl.semaphore_wait(barrier, len(peers))

    state_sum.start()
    w_mine = w_hbm.at[:, pl.ds(pl.multiple_of(core * 512, 512), 512)]
    w_cross = w_hbm.at[:, pl.ds(pl.multiple_of(other * 512, 512), 512)]
    w_slot = w_in.at[z * 2 + core]
    w_copy = [send(w_cross, w_slot, partner)]
    for d in FAR:
        w_copy.append(send(w_mine, w_slot, z_peer(d)))
        w_copy.append(send(w_cross, w_slot, z_cross(d)))
    soft = pl.ds(0, SOFT)
    k_copy = [
        send(k_hbm.at[:, soft], kx.at[0], after),
        send(k_hbm.at[:, soft], kx.at[1], before),
    ]
    v_copy = [
        send(v_hbm.at[:, soft], vx.at[0], after),
        send(v_hbm.at[:, soft], vx.at[1], before),
    ]
    g_copy = [
        send(g_hbm.at[:, pl.ds(pl.multiple_of(other * 512, 512), 512)], g_in, partner)
    ]
    for load in loads[3:]:
        load.wait()

    state_sum.xy()

    row_pos = lax.broadcasted_iota(jnp.int32, (ROWS, ROWS), 0)
    col_pos = lax.broadcasted_iota(jnp.int32, (ROWS, ROWS), 1)
    keep = (col_pos >= row_pos, None, col_pos < row_pos)
    arrived(k_copy)

    def span_of(halo, ref, h):
        return (halo[0, :, head(h)], ref[:, head(h)], halo[1, :, head(h)])

    for h in range(2):
        k_span = span_of(kx, k_ref, h)
        q_h = q_ref[:, head(h)]
        scores = []
        for b in range(3):
            s = dot(q_h, k_span[b], 1, 1) * factor
            scores.append(s if keep[b] is None else jnp.where(keep[b], s, -1e30))
        peak = jnp.max(jnp.maximum(jnp.maximum(scores[0], scores[1]), scores[2]), axis=1, keepdims=True)
        terms = []
        for b in range(3):
            e = jnp.exp(scores[b] - peak)
            terms.append(e if keep[b] is None else jnp.where(keep[b], e, 0.0))
        whole = jnp.sum(terms[0] + terms[1] + terms[2], axis=1, keepdims=True)
        for b in range(3):
            probs[h, b] = terms[b] / whole

    state_sum.along_z()

    arrived(w_copy)
    for i in range(16):
        w_rows[4 * i : 4 * i + 4, :] = w_in[i].astype(F32)

    def w_block(source):
        return w_all.at[core, pl.ds(pl.multiple_of(source * 64, 64), 64), :]

    w_all[core, pl.ds(pl.multiple_of(p * 64, 64), 64), :] = w_rows[...].astype(BF16)
    w_copy = {d: send(w_block(p), w_block(p), xy_peer(d)) for d in FAR}
    w_swap = [send(w_block(p), w_block(p), partner)]

    arrived(v_copy)
    for h in range(2):
        v_span = span_of(vx, v_ref, h)
        total = dot(probs[h, 0].astype(BF16), v_span[0], 1, 0)
        for b in range(1, 3):
            total = total + dot(probs[h, b].astype(BF16), v_span[b], 1, 0)
        attn_own[:, head(h)] = total.astype(BF16)
    a_copy = [send(attn_own.at[:, soft], attn_in.at[:, soft], partner)]

    state_sum.spread()

    arrived(g_copy)
    arrived(a_copy)
    g_mine = g_ref[:, pl.ds(pl.multiple_of(core * 512, 512), 512)]
    wg_soft = Half(0, g_mine, g_in[...])
    wg_soft.xy()

    for d in FAR[::-1]:
        w_copy[d].wait_recv()
        block = w_block((p + 8 - d) % 8)
        w_swap.append(send(block, block, partner))

    state_sum.swap()
    state = state_sum.value()

    phi_q = []
    lin_r = []
    for h in range(2):
        q_lin = q_ref[:, head(2 + h)].astype(F32)
        phi_q.append(unit_plus(q_lin))
        u = dot_wide(phi_q[h], state[h], 1, 0)
        r = lax.rsqrt(jnp.mean(u * u, axis=1, keepdims=True) + norm_eps)
        u_keep[h] = u
        lin_r.append(r)
        attn_own[:, head(2 + h)] = (gain_ref[h : h + 1, :] * u * r).astype(BF16)
    lin = pl.ds(SOFT, SOFT)
    a_copy = [send(attn_own.at[:, lin], attn_in.at[:, lin], partner)]

    arrived(w_swap)
    d_attn = (dot(g_ref[:, 0:512], w_all[0], 1, 1) + dot(g_ref[:, 512:1024], w_all[1], 1, 1)).astype(BF16)

    grad_u = []
    for h in range(2):
        g_lin = gain_ref[h : h + 1, :] * d_attn[:, head(2 + h)].astype(F32)
        u = u_keep[h]
        r = lin_r[h]
        grad_u.append(r * g_lin - u * (r * r * r) * jnp.mean(g_lin * u, axis=1, keepdims=True))
    grad_sum = Total(1, [dot_wide(phi_q[h], grad_u[h], 0, 0) for h in range(2)])
    grad_sum.start()

    arrived(a_copy)
    wg_lin = Half(1, g_mine, g_in[...])
    grad_sum.xy()
    wg_lin.xy()
    wg_soft.along_z()

    for h in range(2):
        k_span = span_of(kx, k_ref, h)
        v_span = span_of(vx, v_ref, h)
        q_h = q_ref[:, head(h)]
        da = d_attn[:, head(h)]
        delta = jnp.sum(da.astype(F32) * attn_own[:, head(h)].astype(F32), axis=1, keepdims=True)
        dq = None
        for b in range(3):
            pr = probs[h, b]
            ds = (pr * (dot(da, v_span[b], 1, 1) - delta)).astype(BF16)
            step = dot(ds, k_span[b], 1, 0)
            dq = step if dq is None else dq + step
            dk = dot(ds, q_h, 0, 0) * factor
            dv = dot(pr.astype(BF16), da, 0, 0)
            if b == 1:
                dkv_keep[0, :, head(h)] = dk
                dkv_keep[1, :, head(h)] = dv
            else:
                back_out[b // 2, 0, :, head(h)] = dk.astype(BF16)
                back_out[b // 2, 1, :, head(h)] = dv.astype(BF16)
        dq_ref[:, head(h)] = (dq * factor).astype(BF16)
    back_copy = [
        send(back_out.at[0], back_in.at[0], before),
        send(back_out.at[1], back_in.at[1], after),
    ]

    grad_sum.along_z()

    for h in range(2):
        q_lin = q_ref[:, head(2 + h)].astype(F32)
        dq_lin = dot_wide(grad_u[h], state[h], 1, 1) * unit_slope(q_lin)
        dq_ref[:, head(2 + h)] = dq_lin.astype(BF16)

    wg_lin.along_z()
    wg_soft.plasmids()
    grad_sum.spread()

    arrived(back_copy)
    for h in range(2):
        for t, out in ((0, dk_ref), (1, dv_ref)):
            total = dkv_keep[t, :, head(h)] + back_in[1, t, :, head(h)].astype(F32)
            total = total + back_in[0, t, :, head(h)].astype(F32)
            out[:, head(h)] = total.astype(BF16)

    wg_lin.plasmids()
    grad_sum.swap()
    dstate = grad_sum.value()
    for h in range(2):
        k_l = k_ref[:, head(2 + h)].astype(F32)
        v_l = v_ref[:, head(2 + h)]
        dk_lin = dot_wide(v_l, dstate[h], 1, 1) * unit_slope(k_l)
        dk_ref[:, head(2 + h)] = dk_lin.astype(BF16)
        dv_ref[:, head(2 + h)] = dot_wide(unit_plus(k_l), dstate[h], 1, 0).astype(BF16)

    wg_soft.value()
    wg_lin.value()
    wg_fin[core, y] = wg_sum[y]
    slot = wg_fin.at[core, y]
    fin_copy = [
        send(wg_sum.at[1 - y], slot, y_peer),
        send(wg_sum.at[1 - y], slot, y_cross),
        send(wg_sum.at[y], slot, partner),
    ]
    arrived(fin_copy)
    for c in range(2):
        for half in range(2):
            rows = wg_fin[c, half]
            first = c * 512 + half * 256
            wg_ref[:, first : first + 256] = jnp.where(core == 0, rows[0:4], rows[4:8])
    for copy in started:
        copy.wait_send()
    assert used[0] == N_COPIES, used[0]


N_COPIES = (
    2 * (1 + 7 + 7 + 7 + 1)
    + 15 + 7 + 8
    + 4 + 1 + 2
    + 2 * (7 + 7 + 3) + 3
    + 2
)


def writer(dq, dk, dv, wg, dq_out, dk_out, dv_out, wg_out, sem):
    copies = [
        pltpu.make_async_copy(src, dst, sem.at[i])
        for i, (src, dst) in enumerate(((dq, dq_out), (dk, dk_out), (dv, dv_out), (wg, wg_out)))
    ]
    for copy in copies:
        copy.start()
    for copy in copies:
        copy.wait()


RESULTS = (((ROWS, 512), BF16), ((ROWS, 512), BF16), ((ROWS, 512), BF16), ((4, 1024), F32))


def body(queries, key_rows, value_rows, out_grad, out_weight, norm_gain):
    vmem = pl.BlockSpec(memory_space=pltpu.VMEM)
    hbm = pl.BlockSpec(memory_space=pltpu.HBM)
    out = pl.pallas_call(
        kernel,
        out_shape=tuple(pltpu.VMEM(*result) for result in RESULTS),
        in_specs=[hbm] * 6,
        out_specs=(vmem,) * 4,
        scratch_shapes=[
            pltpu.VMEM((ROWS, 512), BF16),
            pltpu.VMEM((ROWS, 512), BF16),
            pltpu.VMEM((ROWS, 512), BF16),
            pltpu.VMEM((ROWS, 1024), BF16),
            pltpu.VMEM((4, 1024), BF16),
            pltpu.VMEM((2, DH), F32),
            pltpu.VMEM((2, ROWS, SOFT), BF16),
            pltpu.VMEM((2, ROWS, SOFT), BF16),
            pltpu.VMEM((2, 2, DH, DH), F32),
            pltpu.VMEM((2, DH, DH), F32),
            pltpu.VMEM((2, 8, 16, DH), F32),
            pltpu.VMEM((2, 8, 16, DH), F32),
            pltpu.VMEM((2, 8, 16, DH), F32),
            pltpu.VMEM((2, 2, 8, 16, DH), F32),
            pltpu.VMEM((16, 4, 512), BF16),
            pltpu.VMEM((64, 512), F32),
            pltpu.VMEM((2, 512, 512), BF16),
            pltpu.VMEM((ROWS, 512), BF16),
            pltpu.VMEM((ROWS, 512), BF16),
            pltpu.VMEM((ROWS, 512), BF16),
            pltpu.VMEM((2, 3, ROWS, ROWS), F32),
            pltpu.VMEM((2, ROWS, DH), F32),
            pltpu.VMEM((2, 8, 64, 256), BF16),
            pltpu.VMEM((2, 8, 64, 256), BF16),
            pltpu.VMEM((2, 8, 8, 256), F32),
            pltpu.VMEM((2, 8, 8, 256), F32),
            pltpu.VMEM((2, N_DP, 8, 256), F32),
            pltpu.VMEM((2, 8, 256), F32),
            pltpu.VMEM((2, 2, 8, 256), F32),
            pltpu.VMEM((2, 2, ROWS, SOFT), BF16),
            pltpu.VMEM((2, 2, ROWS, SOFT), BF16),
            pltpu.VMEM((2, ROWS, SOFT), F32),
            pltpu.SemaphoreType.DMA((6,)),
            pltpu.SemaphoreType.DMA((N_COPIES,)),
            pltpu.SemaphoreType.DMA((N_COPIES,)),
        ],
        compiler_params=pltpu.CompilerParams(collective_id=0, has_side_effects=True),
        name="sublayer_backward",
    )(
        queries[0],
        key_rows[0],
        value_rows[0],
        out_grad[0],
        out_weight,
        norm_gain.reshape(2, DH),
    )
    out = pl.pallas_call(
        writer,
        out_shape=tuple(jax.ShapeDtypeStruct(*result) for result in RESULTS),
        in_specs=[vmem] * 4,
        out_specs=(hbm,) * 4,
        scratch_shapes=[pltpu.SemaphoreType.DMA((4,))],
        name="write_out",
    )(*[pltpu.with_memory_space_constraint(x, pltpu.VMEM) for x in out])
    return (out[0][None], out[1][None], out[2][None], out[3])


def solution(mesh):
    return jax.shard_map(
        body,
        mesh=mesh,
        in_specs=(
            P("dp", "seq", None),
            P("dp", "seq", None),
            P("dp", "seq", None),
            P("dp", "seq", None),
            P("seq", None),
            P(),
        ),
        out_specs=(
            P("dp", "seq", None),
            P("dp", "seq", None),
            P("dp", "seq", None),
            P("seq", None),
        ),
        check_vma=False,
    )
```

```python
import math

import jax
import jax.numpy as jnp
from jax import lax
from jax.experimental import pallas as pl
from jax.experimental.pallas import tpu as pltpu
from jax.sharding import PartitionSpec as P

MESH = pl.DeviceIdType.MESH
DH = 128
ROWS = 128
SOFT = 256
N_SEQ = 128
N_DP = 4
norm_eps = 1e-06
BF16 = jnp.bfloat16
F32 = jnp.float32
FAR = (4, 3, 5, 2, 6, 1, 7)


def dot(a, b, a_dim, b_dim):
    return lax.dot_general(a, b, (((a_dim,), (b_dim,)), ((), ())), preferred_element_type=F32)


def parts(x):
    high = x.astype(BF16)
    return high, (x - high.astype(F32)).astype(BF16)


def dot_wide(a, b, a_dim, b_dim):
    if b.dtype == BF16:
        high, low = parts(a)
        return dot(high, b, a_dim, b_dim) + dot(low, b, a_dim, b_dim)
    if a.dtype == BF16:
        high, low = parts(b)
        return dot(a, high, a_dim, b_dim) + dot(a, low, a_dim, b_dim)
    a_high, a_low = parts(a)
    b_high, b_low = parts(b)
    return (
        dot(a_high, b_high, a_dim, b_dim)
        + dot(a_high, b_low, a_dim, b_dim)
        + dot(a_low, b_high, a_dim, b_dim)
    )


def unit_plus(x):
    return jnp.where(x > 0, x + 1.0, jnp.exp(jnp.minimum(x, 0.0)))


def unit_slope(x):
    return jnp.where(x > 0, 1.0, jnp.exp(jnp.minimum(x, 0.0)))


def head(h):
    return slice(h * DH, (h + 1) * DH)


def kernel(
    q_hbm, k_hbm, v_hbm, g_hbm, w_hbm, gain_hbm,
    dq_ref, dk_ref, dv_ref, wg_ref,
    q_ref, k_ref, v_ref, g_ref, w_ref, gain_ref,
    kx, vx, term, term_in, s_one, s_xy, s_z, s_full,
    w_in, w_rows, w_all, g_in, attn_own, attn_in,
    probs, u_keep, wg_out, wg_in, wg_zout, wg_zin, wg_sum, wg_fin,
    back_out, back_in, dkv_keep,
    lsem, ssem, rsem,
):
    dp = lax.axis_index("dp")
    seq = lax.axis_index("seq")
    core = seq % 2
    z = (seq // 2) % 8
    p = seq // 16
    y = p // 4
    other = 1 - core
    partner = seq + 1 - 2 * core
    after = (seq + 1) % N_SEQ
    before = (seq + N_SEQ - 1) % N_SEQ
    factor = DH ** (-0.5)

    loads = [
        pltpu.make_async_copy(src, dst, lsem.at[i])
        for i, (src, dst) in enumerate(
            (
                (k_hbm, k_ref),
                (v_hbm, v_ref),
                (w_hbm, w_ref),
                (q_hbm, q_ref),
                (gain_hbm, gain_ref),
                (g_hbm, g_ref),
            )
        )
    ]
    for load in loads:
        load.start()

    def xy_peer(d):
        return (((p + d) % 8) * 8 + z) * 2 + core

    def z_peer(d):
        return (p * 8 + (z + d) % 8) * 2 + core

    def z_cross(d):
        return (p * 8 + (z + d) % 8) * 2 + other

    def column_peer(step):
        to_dp, flip, cross = step
        chip = ((p + 4 * flip) % 8) * 8 + z
        return (dp + to_dp) % N_DP, chip * 2 + (core + cross) % 2

    steps = [(a, b, c) for a in (2, 1, 3, 0) for b in range(2) for c in range(2)][:-4]
    steps += [(0, 1, 1), (0, 1, 0), (0, 0, 1)]

    barrier = pltpu.get_barrier_semaphore()
    peers = [column_peer(step) for step in steps]
    peers += [(dp, z_peer(d)) for d in FAR]
    peers += [(dp, z_cross(d)) for d in FAR]
    peers += [(dp, xy_peer(d)) for d in FAR]
    peers += [(dp, after), (dp, before)]
    for peer in peers:
        pl.semaphore_signal(barrier, inc=1, device_id=peer, device_id_type=MESH)

    used = [0]
    started = []
    fin_base = N_COPIES

    def send(src, dst, device, dp_to=None):
        index = used[0]
        used[0] += 1
        copy = pltpu.make_async_remote_copy(
            src_ref=src,
            dst_ref=dst,
            send_sem=ssem.at[index],
            recv_sem=rsem.at[index],
            device_id=(dp if dp_to is None else dp_to, device),
            device_id_type=MESH,
        )
        copy.start()
        started.append(copy)
        return copy

    def arrived(copies):
        for copy in copies:
            copy.wait_recv()

    class Total:
        def __init__(self, slot, terms):
            self.i = slot
            for h in range(2):
                term[slot, h] = terms[h]

        def start(self):
            i = self.i
            self.c = [send(term.at[i, other], term_in.at[i], partner)]

        def xy(self):
            i = self.i
            arrived(self.c)
            s_one[i] = (term[i, core] + term_in[i]).reshape(8, 16, DH)
            self.c = [send(s_one.at[i, (p + d) % 8], s_xy.at[i, d], xy_peer(d)) for d in FAR]

        def along_z(self):
            i = self.i
            arrived(self.c)
            total = s_one[i, p]
            for d in range(1, 8):
                total = total + s_xy[i, d]
            s_z[i, z] = total
            self.c = [send(s_z.at[i, z], s_z.at[i, z], z_peer(d)) for d in FAR]

        def spread(self):
            i = self.i
            arrived(self.c)
            total = s_z[i, 0]
            for d in range(1, 8):
                total = total + s_z[i, d]
            s_full[i, core, p] = total
            mine = s_full.at[i, core, p]
            self.c = [send(mine, mine, xy_peer(d)) for d in FAR]

        def swap(self):
            i = self.i
            arrived(self.c)
            mine = s_full.at[i, core]
            self.c = [send(mine, mine, partner)]

        def value(self):
            arrived(self.c)
            return [s_full[self.i, h].reshape(DH, DH) for h in range(2)]

    class Half:
        def __init__(self, half, g_mine, g_other):
            self.s = s = half
            for b in range(4):
                rows = slice(s * SOFT + b * 64, s * SOFT + (b + 1) * 64)
                block = dot(attn_own[:, rows], g_mine, 0, 0) + dot(attn_in[:, rows], g_other, 0, 0)
                block = block.astype(BF16)
                wg_out[s, b] = block[:, 0:256]
                wg_out[s, 4 + b] = block[:, 256:512]

        def xy(self):
            s = self.s
            self.c = [send(wg_out.at[s, (p + d) % 8], wg_in.at[s, d], xy_peer(d)) for d in FAR]

        def along_z(self):
            s = self.s
            arrived(self.c)
            total = wg_out[s, p].astype(F32)
            for d in range(1, 8):
                total = total + wg_in[s, d].astype(F32)
            wg_zout[s] = total.reshape(8, 8, 256)
            self.c = [send(wg_zout.at[s, (z + d) % 8], wg_zin.at[s, d], z_peer(d)) for d in FAR]

        def deliver(self):
            s = self.s
            arrived(self.c)
            total = wg_zout[s, z]
            for d in range(1, 8):
                total = total + wg_zin[s, d]
            for c in range(2):
                wg_sum[s, c] = total[4 * c : 4 * c + 4]
            flip = (s + y) % 2
            owner = ((s * 4 + p % 4) * 8 + z) * 2

            def copy_to(to_dp, cross):
                index = fin_base + flip * 8 + to_dp * 2 + cross
                core_to = (core + cross) % 2
                return pltpu.make_async_remote_copy(
                    src_ref=wg_sum.at[s, core_to],
                    dst_ref=wg_fin.at[dp, core, y],
                    send_sem=ssem.at[index],
                    recv_sem=rsem.at[index],
                    device_id=((dp + to_dp) % N_DP, owner + core_to),
                    device_id_type=MESH,
                )

            self.out = [copy_to(a, c) for a in (2, 1, 3) for c in range(2)] + [copy_to(0, 1)]
            for copy in self.out:
                copy.start()
            self.last = copy_to(0, 0)

            @pl.when(flip == 1)
            def _():
                self.last.start()

            @pl.when(flip == 0)
            def _():
                wg_fin[dp, core, y] = wg_sum[s, core]

        def finish(self):
            for copy in self.out:
                copy.wait_send()

            @pl.when((self.s + y) % 2 == 1)
            def _():
                self.last.wait_send()

    loads[0].wait()
    loads[1].wait()
    state_sum = Total(
        0,
        [
            dot_wide(unit_plus(k_ref[:, head(2 + h)].astype(F32)), v_ref[:, head(2 + h)], 0, 0)
            for h in range(2)
        ],
    )
    loads[2].wait()
    w_in[z * 2 + core] = jnp.where(
        core == 0, w_ref[:, 0:512].astype(F32), w_ref[:, 512:1024].astype(F32)
    ).astype(BF16)

    pl.semaphore_wait(barrier, len(peers))

    state_sum.start()
    w_mine = w_hbm.at[:, pl.ds(pl.multiple_of(core * 512, 512), 512)]
    w_cross = w_hbm.at[:, pl.ds(pl.multiple_of(other * 512, 512), 512)]
    w_slot = w_in.at[z * 2 + core]
    w_copy = [send(w_cross, w_slot, partner)]
    for d in FAR:
        w_copy.append(send(w_mine, w_slot, z_peer(d)))
        w_copy.append(send(w_cross, w_slot, z_cross(d)))
    soft = pl.ds(0, SOFT)
    k_copy = [
        send(k_hbm.at[:, soft], kx.at[0], after),
        send(k_hbm.at[:, soft], kx.at[1], before),
    ]
    v_copy = [
        send(v_hbm.at[:, soft], vx.at[0], after),
        send(v_hbm.at[:, soft], vx.at[1], before),
    ]
    g_copy = [
        send(g_hbm.at[:, pl.ds(pl.multiple_of(other * 512, 512), 512)], g_in, partner)
    ]
    for load in loads[3:]:
        load.wait()

    state_sum.xy()

    row_pos = lax.broadcasted_iota(jnp.int32, (ROWS, ROWS), 0)
    col_pos = lax.broadcasted_iota(jnp.int32, (ROWS, ROWS), 1)
    keep = (col_pos >= row_pos, None, col_pos < row_pos)
    arrived(k_copy)

    def span_of(halo, ref, h):
        return (halo[0, :, head(h)], ref[:, head(h)], halo[1, :, head(h)])

    for h in range(2):
        k_span = span_of(kx, k_ref, h)
        q_h = q_ref[:, head(h)]
        scores = []
        for b in range(3):
            s = dot(q_h, k_span[b], 1, 1) * factor
            scores.append(s if keep[b] is None else jnp.where(keep[b], s, -1e30))
        peak = jnp.max(jnp.maximum(jnp.maximum(scores[0], scores[1]), scores[2]), axis=1, keepdims=True)
        terms = []
        for b in range(3):
            e = jnp.exp(scores[b] - peak)
            terms.append(e if keep[b] is None else jnp.where(keep[b], e, 0.0))
        whole = jnp.sum(terms[0] + terms[1] + terms[2], axis=1, keepdims=True)
        for b in range(3):
            probs[h, b] = terms[b] / whole

    state_sum.along_z()

    arrived(w_copy)
    for i in range(16):
        w_rows[4 * i : 4 * i + 4, :] = w_in[i].astype(F32)

    def w_block(source):
        return w_all.at[core, pl.ds(pl.multiple_of(source * 64, 64), 64), :]

    w_all[core, pl.ds(pl.multiple_of(p * 64, 64), 64), :] = w_rows[...].astype(BF16)
    w_copy = {d: send(w_block(p), w_block(p), xy_peer(d)) for d in FAR}
    w_swap = [send(w_block(p), w_block(p), partner)]

    arrived(v_copy)
    for h in range(2):
        v_span = span_of(vx, v_ref, h)
        total = dot(probs[h, 0].astype(BF16), v_span[0], 1, 0)
        for b in range(1, 3):
            total = total + dot(probs[h, b].astype(BF16), v_span[b], 1, 0)
        attn_own[:, head(h)] = total.astype(BF16)
    a_copy = [send(attn_own.at[:, soft], attn_in.at[:, soft], partner)]

    state_sum.spread()

    arrived(g_copy)
    arrived(a_copy)
    g_mine = g_ref[:, pl.ds(pl.multiple_of(core * 512, 512), 512)]
    wg_soft = Half(0, g_mine, g_in[...])
    wg_soft.xy()

    for d in FAR[::-1]:
        w_copy[d].wait_recv()
        block = w_block((p + 8 - d) % 8)
        w_swap.append(send(block, block, partner))

    state_sum.swap()
    state = state_sum.value()

    phi_q = []
    lin_r = []
    for h in range(2):
        q_lin = q_ref[:, head(2 + h)].astype(F32)
        phi_q.append(unit_plus(q_lin))
        u = dot_wide(phi_q[h], state[h], 1, 0)
        r = lax.rsqrt(jnp.mean(u * u, axis=1, keepdims=True) + norm_eps)
        u_keep[h] = u
        lin_r.append(r)
        attn_own[:, head(2 + h)] = (gain_ref[h : h + 1, :] * u * r).astype(BF16)
    lin = pl.ds(SOFT, SOFT)
    a_copy = [send(attn_own.at[:, lin], attn_in.at[:, lin], partner)]

    mine_lin = dot(g_mine, w_all[core, SOFT:512, :], 1, 1)
    arrived(a_copy)
    wg_lin = Half(1, g_mine, g_in[...])
    wg_lin.xy()

    arrived(w_swap)
    g_cross = g_ref[:, pl.ds(pl.multiple_of(other * 512, 512), 512)]
    d_attn_lin = (mine_lin + dot(g_cross, w_all[other, SOFT:512, :], 1, 1)).astype(BF16)

    grad_u = []
    for h in range(2):
        g_lin = gain_ref[h : h + 1, :] * d_attn_lin[:, head(h)].astype(F32)
        u = u_keep[h]
        r = lin_r[h]
        grad_u.append(r * g_lin - u * (r * r * r) * jnp.mean(g_lin * u, axis=1, keepdims=True))
    grad_sum = Total(1, [dot_wide(phi_q[h], grad_u[h], 0, 0) for h in range(2)])
    grad_sum.start()

    d_attn = dot(g_ref[:, 0:512], w_all[0, 0:SOFT, :], 1, 1) + dot(g_ref[:, 512:1024], w_all[1, 0:SOFT, :], 1, 1)
    d_attn = d_attn.astype(BF16)
    grad_sum.xy()
    wg_soft.along_z()

    for h in range(2):
        k_span = span_of(kx, k_ref, h)
        v_span = span_of(vx, v_ref, h)
        q_h = q_ref[:, head(h)]
        da = d_attn[:, head(h)]
        delta = jnp.sum(da.astype(F32) * attn_own[:, head(h)].astype(F32), axis=1, keepdims=True)
        dq = None
        for b in range(3):
            pr = probs[h, b]
            ds = (pr * (dot(da, v_span[b], 1, 1) - delta)).astype(BF16)
            step = dot(ds, k_span[b], 1, 0)
            dq = step if dq is None else dq + step
            dk = dot(ds, q_h, 0, 0) * factor
            dv = dot(pr.astype(BF16), da, 0, 0)
            if b == 1:
                dkv_keep[0, :, head(h)] = dk
                dkv_keep[1, :, head(h)] = dv
            else:
                back_out[b // 2, 0, :, head(h)] = dk.astype(BF16)
                back_out[b // 2, 1, :, head(h)] = dv.astype(BF16)
        dq_ref[:, head(h)] = (dq * factor).astype(BF16)
    back_copy = [
        send(back_out.at[0], back_in.at[0], before),
        send(back_out.at[1], back_in.at[1], after),
    ]

    grad_sum.along_z()

    for h in range(2):
        q_lin = q_ref[:, head(2 + h)].astype(F32)
        dq_lin = dot_wide(grad_u[h], state[h], 1, 1) * unit_slope(q_lin)
        dq_ref[:, head(2 + h)] = dq_lin.astype(BF16)

    wg_lin.along_z()
    wg_soft.deliver()
    grad_sum.spread()

    arrived(back_copy)
    for h in range(2):
        for t, out in ((0, dk_ref), (1, dv_ref)):
            total = dkv_keep[t, :, head(h)] + back_in[1, t, :, head(h)].astype(F32)
            total = total + back_in[0, t, :, head(h)].astype(F32)
            out[:, head(h)] = total.astype(BF16)

    wg_lin.deliver()
    grad_sum.swap()
    dstate = grad_sum.value()
    for h in range(2):
        k_l = k_ref[:, head(2 + h)].astype(F32)
        v_l = v_ref[:, head(2 + h)]
        dk_lin = dot_wide(v_l, dstate[h], 1, 1) * unit_slope(k_l)
        dk_ref[:, head(2 + h)] = dk_lin.astype(BF16)
        dv_ref[:, head(2 + h)] = dot_wide(unit_plus(k_l), dstate[h], 1, 0).astype(BF16)

    for step in steps:
        to_dp, flip, cross = step
        index = fin_base + flip * 8 + to_dp * 2 + cross
        pltpu.make_async_remote_copy(
            src_ref=wg_sum.at[0, 0],
            dst_ref=wg_fin.at[0, 0, 0],
            send_sem=ssem.at[index],
            recv_sem=rsem.at[index],
            device_id=column_peer(step),
            device_id_type=MESH,
        ).wait_recv()
    for c in range(2):
        for half in range(2):
            total = (wg_fin[0, c, half] + wg_fin[1, c, half]) + (wg_fin[2, c, half] + wg_fin[3, c, half])
            first = c * 512 + half * 256
            wg_ref[:, first : first + 256] = total * (1.0 / math.sqrt(N_DP * N_SEQ * ROWS))
    wg_soft.finish()
    wg_lin.finish()
    for copy in started:
        copy.wait_send()
    assert used[0] == N_COPIES, used[0]


N_COPIES = (
    2 * (1 + 7 + 7 + 7 + 1)
    + 15 + 7 + 8
    + 4 + 1 + 2
    + 2 * (7 + 7)
    + 2
)


def writer(dq, dk, dv, wg, dq_out, dk_out, dv_out, wg_out, sem):
    copies = [
        pltpu.make_async_copy(src, dst, sem.at[i])
        for i, (src, dst) in enumerate(((dq, dq_out), (dk, dk_out), (dv, dv_out), (wg, wg_out)))
    ]
    for copy in copies:
        copy.start()
    for copy in copies:
        copy.wait()


RESULTS = (((ROWS, 512), BF16), ((ROWS, 512), BF16), ((ROWS, 512), BF16), ((4, 1024), F32))


def body(queries, key_rows, value_rows, out_grad, out_weight, norm_gain):
    vmem = pl.BlockSpec(memory_space=pltpu.VMEM)
    hbm = pl.BlockSpec(memory_space=pltpu.HBM)
    out = pl.pallas_call(
        kernel,
        out_shape=tuple(pltpu.VMEM(*result) for result in RESULTS),
        in_specs=[hbm] * 6,
        out_specs=(vmem,) * 4,
        scratch_shapes=[
            pltpu.VMEM((ROWS, 512), BF16),
            pltpu.VMEM((ROWS, 512), BF16),
            pltpu.VMEM((ROWS, 512), BF16),
            pltpu.VMEM((ROWS, 1024), BF16),
            pltpu.VMEM((4, 1024), BF16),
            pltpu.VMEM((2, DH), F32),
            pltpu.VMEM((2, ROWS, SOFT), BF16),
            pltpu.VMEM((2, ROWS, SOFT), BF16),
            pltpu.VMEM((2, 2, DH, DH), F32),
            pltpu.VMEM((2, DH, DH), F32),
            pltpu.VMEM((2, 8, 16, DH), F32),
            pltpu.VMEM((2, 8, 16, DH), F32),
            pltpu.VMEM((2, 8, 16, DH), F32),
            pltpu.VMEM((2, 2, 8, 16, DH), F32),
            pltpu.VMEM((16, 4, 512), BF16),
            pltpu.VMEM((64, 512), F32),
            pltpu.VMEM((2, 512, 512), BF16),
            pltpu.VMEM((ROWS, 512), BF16),
            pltpu.VMEM((ROWS, 512), BF16),
            pltpu.VMEM((ROWS, 512), BF16),
            pltpu.VMEM((2, 3, ROWS, ROWS), F32),
            pltpu.VMEM((2, ROWS, DH), F32),
            pltpu.VMEM((2, 8, 64, 256), BF16),
            pltpu.VMEM((2, 8, 64, 256), BF16),
            pltpu.VMEM((2, 8, 8, 256), F32),
            pltpu.VMEM((2, 8, 8, 256), F32),
            pltpu.VMEM((2, 2, 4, 256), F32),
            pltpu.VMEM((N_DP, 2, 2, 4, 256), F32),
            pltpu.VMEM((2, 2, ROWS, SOFT), BF16),
            pltpu.VMEM((2, 2, ROWS, SOFT), BF16),
            pltpu.VMEM((2, ROWS, SOFT), F32),
            pltpu.SemaphoreType.DMA((6,)),
            pltpu.SemaphoreType.DMA((N_COPIES + 16,)),
            pltpu.SemaphoreType.DMA((N_COPIES + 16,)),
        ],
        compiler_params=pltpu.CompilerParams(collective_id=0, has_side_effects=True),
        name="sublayer_backward",
    )(
        queries[0],
        key_rows[0],
        value_rows[0],
        out_grad[0],
        out_weight,
        norm_gain.reshape(2, DH),
    )
    out = pl.pallas_call(
        writer,
        out_shape=tuple(jax.ShapeDtypeStruct(*result) for result in RESULTS),
        in_specs=[vmem] * 4,
        out_specs=(hbm,) * 4,
        scratch_shapes=[pltpu.SemaphoreType.DMA((4,))],
        name="write_out",
    )(*[pltpu.with_memory_space_constraint(x, pltpu.VMEM) for x in out])
    return (out[0][None], out[1][None], out[2][None], out[3])


def solution(mesh):
    return jax.shard_map(
        body,
        mesh=mesh,
        in_specs=(
            P("dp", "seq", None),
            P("dp", "seq", None),
            P("dp", "seq", None),
            P("dp", "seq", None),
            P("seq", None),
            P(),
        ),
        out_specs=(
            P("dp", "seq", None),
            P("dp", "seq", None),
            P("dp", "seq", None),
            P("seq", None),
        ),
        check_vma=False,
    )
```

```python
import math

import jax
import jax.numpy as jnp
from jax import lax
from jax.experimental import pallas as pl
from jax.experimental.pallas import tpu as pltpu
from jax.sharding import PartitionSpec as P

MESH = pl.DeviceIdType.MESH
DH = 128
ROWS = 128
SOFT = 256
N_SEQ = 128
N_DP = 4
norm_eps = 1e-06
BF16 = jnp.bfloat16
F32 = jnp.float32
FAR = (4, 3, 5, 2, 6, 1, 7)


def dot(a, b, a_dim, b_dim):
    return lax.dot_general(a, b, (((a_dim,), (b_dim,)), ((), ())), preferred_element_type=F32)


def parts(x):
    high = x.astype(BF16)
    return high, (x - high.astype(F32)).astype(BF16)


def dot_wide(a, b, a_dim, b_dim):
    if b.dtype == BF16:
        high, low = parts(a)
        return dot(high, b, a_dim, b_dim) + dot(low, b, a_dim, b_dim)
    if a.dtype == BF16:
        high, low = parts(b)
        return dot(a, high, a_dim, b_dim) + dot(a, low, a_dim, b_dim)
    a_high, a_low = parts(a)
    b_high, b_low = parts(b)
    return (
        dot(a_high, b_high, a_dim, b_dim)
        + dot(a_high, b_low, a_dim, b_dim)
        + dot(a_low, b_high, a_dim, b_dim)
    )


def unit_plus(x):
    return jnp.where(x > 0, x + 1.0, jnp.exp(jnp.minimum(x, 0.0)))


def unit_slope(x):
    return jnp.where(x > 0, 1.0, jnp.exp(jnp.minimum(x, 0.0)))


def head(h):
    return slice(h * DH, (h + 1) * DH)


def kernel(
    q_hbm, k_hbm, v_hbm, g_hbm, w_hbm, gain_hbm,
    dq_ref, dk_ref, dv_ref, wg_ref,
    q_ref, k_ref, v_ref, g_ref, w_ref, gain_ref,
    kx, vx, phi_part, phi_turned, term, s_xy, s_z, s_full,
    w_in, w_rows, w_all, g_in, attn_own, attn_in,
    probs, u_keep, wg_out, wg_in, wg_zout, wg_zin, wg_sum, wg_fin,
    back_out, back_in, dkv_keep,
    lsem, ssem, rsem,
):
    dp = lax.axis_index("dp")
    seq = lax.axis_index("seq")
    core = seq % 2
    z = (seq // 2) % 8
    p = seq // 16
    y = p // 4
    other = 1 - core
    partner = seq + 1 - 2 * core
    after = (seq + 1) % N_SEQ
    before = (seq + N_SEQ - 1) % N_SEQ
    factor = DH ** (-0.5)

    loads = [
        pltpu.make_async_copy(src, dst, lsem.at[i])
        for i, (src, dst) in enumerate(
            (
                (k_hbm, k_ref),
                (v_hbm, v_ref),
                (w_hbm, w_ref),
                (q_hbm, q_ref),
                (gain_hbm, gain_ref),
                (g_hbm, g_ref),
            )
        )
    ]
    for load in loads:
        load.start()

    def xy_peer(d):
        return (((p + d) % 8) * 8 + z) * 2 + core

    def flat_peer(d, cross):
        return (((p + d) % 8) * 8 + z) * 2 + (core + cross) % 2

    def z_peer(d):
        return (p * 8 + (z + d) % 8) * 2 + core

    def z_cross(d):
        return (p * 8 + (z + d) % 8) * 2 + other

    def column_peer(step):
        to_dp, flip, cross = step
        chip = ((p + 4 * flip) % 8) * 8 + z
        return (dp + to_dp) % N_DP, chip * 2 + (core + cross) % 2

    steps = [(a, b, c) for a in (2, 1, 3, 0) for b in range(2) for c in range(2)][:-4]
    steps += [(0, 1, 1), (0, 1, 0), (0, 0, 1)]

    barrier = pltpu.get_barrier_semaphore()
    peers = [column_peer(step) for step in steps]
    peers += [(dp, z_peer(d)) for d in FAR]
    peers += [(dp, z_cross(d)) for d in FAR]
    peers += [(dp, flat_peer(d, cross)) for d in FAR if d != 4 for cross in range(2)]
    peers += [(dp, after), (dp, before)]
    for peer in peers:
        pl.semaphore_signal(barrier, inc=1, device_id=peer, device_id_type=MESH)

    used = [0]
    started = []
    fin_base = N_COPIES

    def send(src, dst, device, dp_to=None):
        index = used[0]
        used[0] += 1
        copy = pltpu.make_async_remote_copy(
            src_ref=src,
            dst_ref=dst,
            send_sem=ssem.at[index],
            recv_sem=rsem.at[index],
            device_id=(dp if dp_to is None else dp_to, device),
            device_id_type=MESH,
        )
        copy.start()
        started.append(copy)
        return copy

    def arrived(copies):
        for copy in copies:
            copy.wait_recv()

    near = [(d, cross) for d in FAR for cross in range(2)] + [(0, 1)]

    class Total:
        def __init__(self, slot, terms):
            self.i = slot
            for h in range(2):
                term[slot, h] = terms[h].astype(BF16).reshape(8, 16, DH)

        def start(self):
            i = self.i
            self.c = [
                send(term.at[i, (core + cross) % 2, (p + d) % 8], s_xy.at[i, d, cross], flat_peer(d, cross))
                for d, cross in near
            ]

        def along_z(self):
            i = self.i
            arrived(self.c)
            total = term[i, core, p].astype(F32)
            for d, cross in near[::-1]:
                total = total + s_xy[i, d, cross].astype(F32)
            s_z[i, z] = total.astype(BF16)
            self.c = [send(s_z.at[i, z], s_z.at[i, z], z_peer(d)) for d in FAR]

        def spread(self):
            i = self.i
            arrived(self.c)
            total = s_z[i, 0].astype(F32)
            for d in range(1, 8):
                total = total + s_z[i, d].astype(F32)
            s_full[i, core, p] = total.astype(BF16)
            mine = s_full.at[i, core, p]
            self.c = [send(mine, mine, flat_peer(d, cross)) for d, cross in near]

        def value(self):
            arrived(self.c)
            return [s_full[self.i, h].reshape(DH, DH) for h in range(2)]

    class Half:
        def __init__(self, half, g_mine, g_other):
            self.s = s = half
            for b in range(4):
                rows = slice(s * SOFT + b * 64, s * SOFT + (b + 1) * 64)
                block = dot(attn_own[:, rows], g_mine, 0, 0) + dot(attn_in[:, rows], g_other, 0, 0)
                block = block.astype(BF16)
                wg_out[s, b] = block[:, 0:256]
                wg_out[s, 4 + b] = block[:, 256:512]

        def xy(self):
            s = self.s
            self.c = [send(wg_out.at[s, (p + d) % 8], wg_in.at[s, d], xy_peer(d)) for d in FAR]

        def along_z(self):
            s = self.s
            arrived(self.c)
            total = wg_out[s, p].astype(F32)
            for d in range(1, 8):
                total = total + wg_in[s, d].astype(F32)
            wg_zout[s] = total.reshape(8, 8, 256).astype(BF16)
            self.c = [send(wg_zout.at[s, (z + d) % 8], wg_zin.at[s, d], z_peer(d)) for d in FAR]

        def deliver(self):
            s = self.s
            arrived(self.c)
            total = wg_zout[s, z].astype(F32)
            for d in range(1, 8):
                total = total + wg_zin[s, d].astype(F32)
            for c in range(2):
                wg_sum[s, c] = total[4 * c : 4 * c + 4]
            flip = (s + y) % 2
            owner = ((s * 4 + p % 4) * 8 + z) * 2

            def copy_to(to_dp, cross):
                index = fin_base + flip * 8 + to_dp * 2 + cross
                core_to = (core + cross) % 2
                return pltpu.make_async_remote_copy(
                    src_ref=wg_sum.at[s, core_to],
                    dst_ref=wg_fin.at[dp, core, y],
                    send_sem=ssem.at[index],
                    recv_sem=rsem.at[index],
                    device_id=((dp + to_dp) % N_DP, owner + core_to),
                    device_id_type=MESH,
                )

            self.out = [copy_to(a, c) for a in (2, 1, 3) for c in range(2)] + [copy_to(0, 1)]
            for copy in self.out:
                copy.start()
            self.last = copy_to(0, 0)

            @pl.when(flip == 1)
            def _():
                self.last.start()

            @pl.when(flip == 0)
            def _():
                wg_fin[dp, core, y] = wg_sum[s, core]

        def finish(self):
            for copy in self.out:
                copy.wait_send()

            @pl.when((self.s + y) % 2 == 1)
            def _():
                self.last.wait_send()

    loads[0].wait()
    loads[1].wait()
    state_sum = Total(
        0,
        [
            dot_wide(unit_plus(k_ref[:, head(2 + h)].astype(F32)), v_ref[:, head(2 + h)], 0, 0)
            for h in range(2)
        ],
    )
    loads[2].wait()
    w_in[z * 2 + core] = jnp.where(
        core == 0, w_ref[:, 0:512].astype(F32), w_ref[:, 512:1024].astype(F32)
    ).astype(BF16)

    pl.semaphore_wait(barrier, len(peers))

    state_sum.start()
    w_mine = w_hbm.at[:, pl.ds(pl.multiple_of(core * 512, 512), 512)]
    w_cross = w_hbm.at[:, pl.ds(pl.multiple_of(other * 512, 512), 512)]
    w_slot = w_in.at[z * 2 + core]
    w_copy = [send(w_cross, w_slot, partner)]
    for d in FAR:
        w_copy.append(send(w_mine, w_slot, z_peer(d)))
        w_copy.append(send(w_cross, w_slot, z_cross(d)))
    soft = pl.ds(0, SOFT)
    k_copy = [
        send(k_hbm.at[:, soft], kx.at[0], after),
        send(k_hbm.at[:, soft], kx.at[1], before),
    ]
    v_copy = [
        send(v_hbm.at[:, soft], vx.at[0], after),
        send(v_hbm.at[:, soft], vx.at[1], before),
    ]
    g_copy = [
        send(g_hbm.at[:, pl.ds(pl.multiple_of(other * 512, 512), 512)], g_in, partner)
    ]
    for load in loads[3:]:
        load.wait()

    for h in range(2):
        for i, part in enumerate(parts(unit_plus(q_ref[:, head(2 + h)].astype(F32)))):
            phi_part[h, i] = part
            phi_turned[h, i] = part.T

    state_sum.along_z()

    arrived(w_copy)
    for i in range(16):
        w_rows[4 * i : 4 * i + 4, :] = w_in[i].astype(F32)

    def w_block(source):
        return w_all.at[core, pl.ds(pl.multiple_of(source * 64, 64), 64), :]

    w_all[core, pl.ds(pl.multiple_of(p * 64, 64), 64), :] = w_rows[...].astype(BF16)
    w_copy = {d: send(w_block(p), w_block(p), xy_peer(d)) for d in FAR}
    w_swap = [send(w_block(p), w_block(p), partner)]

    row_pos = lax.broadcasted_iota(jnp.int32, (ROWS, ROWS), 0)
    col_pos = lax.broadcasted_iota(jnp.int32, (ROWS, ROWS), 1)
    keep = (col_pos >= row_pos, None, col_pos < row_pos)
    arrived(k_copy)

    def span_of(halo, ref, h):
        return (halo[0, :, head(h)], ref[:, head(h)], halo[1, :, head(h)])

    for h in range(2):
        k_span = span_of(kx, k_ref, h)
        q_h = q_ref[:, head(h)]
        scores = []
        for b in range(3):
            s = dot(q_h, k_span[b], 1, 1) * factor
            scores.append(s if keep[b] is None else jnp.where(keep[b], s, -1e30))
        peak = jnp.max(jnp.maximum(jnp.maximum(scores[0], scores[1]), scores[2]), axis=1, keepdims=True)
        terms = []
        for b in range(3):
            e = jnp.exp(scores[b] - peak)
            terms.append(e if keep[b] is None else jnp.where(keep[b], e, 0.0))
        whole = jnp.sum(terms[0] + terms[1] + terms[2], axis=1, keepdims=True)
        for b in range(3):
            probs[h, b] = terms[b] / whole

    arrived(v_copy)
    for h in range(2):
        v_span = span_of(vx, v_ref, h)
        total = dot(probs[h, 0].astype(BF16), v_span[0], 1, 0)
        for b in range(1, 3):
            total = total + dot(probs[h, b].astype(BF16), v_span[b], 1, 0)
        attn_own[:, head(h)] = total.astype(BF16)
    a_copy = [send(attn_own.at[:, soft], attn_in.at[:, soft], partner)]

    state_sum.spread()

    arrived(g_copy)
    arrived(a_copy)
    g_mine = g_ref[:, pl.ds(pl.multiple_of(core * 512, 512), 512)]
    wg_soft = Half(0, g_mine, g_in[...])
    wg_soft.xy()

    for d in FAR[::-1]:
        w_copy[d].wait_recv()
        block = w_block((p + 8 - d) % 8)
        w_swap.append(send(block, block, partner))

    state = state_sum.value()

    lin_r = []
    for h in range(2):
        u = dot(phi_part[h, 0], state[h], 1, 0) + dot(phi_part[h, 1], state[h], 1, 0)
        r = lax.rsqrt(jnp.mean(u * u, axis=1, keepdims=True) + norm_eps)
        u_keep[h] = u
        lin_r.append(r)
        attn_own[:, head(2 + h)] = (gain_ref[h : h + 1, :] * u * r).astype(BF16)
    lin = pl.ds(SOFT, SOFT)
    a_copy = [send(attn_own.at[:, lin], attn_in.at[:, lin], partner)]

    mine_lin = dot(g_mine, w_all[core, SOFT:512, :], 1, 1)
    arrived(w_swap)
    g_cross = g_ref[:, pl.ds(pl.multiple_of(other * 512, 512), 512)]
    d_attn_lin = (mine_lin + dot(g_cross, w_all[other, SOFT:512, :], 1, 1)).astype(BF16)

    grad_u = []
    for h in range(2):
        g_lin = gain_ref[h : h + 1, :] * d_attn_lin[:, head(h)].astype(F32)
        u = u_keep[h]
        r = lin_r[h]
        grad_u.append(r * g_lin - u * (r * r * r) * jnp.mean(g_lin * u, axis=1, keepdims=True))
    terms = []
    for h in range(2):
        high, low = parts(grad_u[h])
        terms.append(
            dot(phi_turned[h, 0], high, 1, 0) + dot(phi_turned[h, 0], low, 1, 0) + dot(phi_turned[h, 1], high, 1, 0)
        )
    grad_sum = Total(1, terms)
    grad_sum.start()

    arrived(a_copy)
    wg_lin = Half(1, g_mine, g_in[...])
    wg_lin.xy()
    d_attn = dot(g_ref[:, 0:512], w_all[0, 0:SOFT, :], 1, 1) + dot(g_ref[:, 512:1024], w_all[1, 0:SOFT, :], 1, 1)
    d_attn = d_attn.astype(BF16)
    wg_soft.along_z()

    for h in range(2):
        k_span = span_of(kx, k_ref, h)
        v_span = span_of(vx, v_ref, h)
        q_h = q_ref[:, head(h)]
        da = d_attn[:, head(h)]
        delta = jnp.sum(da.astype(F32) * attn_own[:, head(h)].astype(F32), axis=1, keepdims=True)
        dq = None
        for b in range(3):
            pr = probs[h, b]
            ds = (pr * (dot(da, v_span[b], 1, 1) - delta)).astype(BF16)
            step = dot(ds, k_span[b], 1, 0)
            dq = step if dq is None else dq + step
            dk = dot(ds, q_h, 0, 0) * factor
            dv = dot(pr.astype(BF16), da, 0, 0)
            if b == 1:
                dkv_keep[0, :, head(h)] = dk
                dkv_keep[1, :, head(h)] = dv
            else:
                back_out[b // 2, 0, :, head(h)] = dk.astype(BF16)
                back_out[b // 2, 1, :, head(h)] = dv.astype(BF16)
        dq_ref[:, head(h)] = (dq * factor).astype(BF16)
    grad_sum.along_z()

    back_copy = [
        send(back_out.at[0], back_in.at[0], before),
        send(back_out.at[1], back_in.at[1], after),
    ]

    for h in range(2):
        q_lin = q_ref[:, head(2 + h)].astype(F32)
        dq_lin = dot_wide(grad_u[h], state[h], 1, 1) * unit_slope(q_lin)
        dq_ref[:, head(2 + h)] = dq_lin.astype(BF16)

    wg_lin.along_z()
    wg_soft.deliver()
    grad_sum.spread()

    arrived(back_copy)
    for h in range(2):
        for t, out in ((0, dk_ref), (1, dv_ref)):
            total = dkv_keep[t, :, head(h)] + back_in[1, t, :, head(h)].astype(F32)
            total = total + back_in[0, t, :, head(h)].astype(F32)
            out[:, head(h)] = total.astype(BF16)

    wg_lin.deliver()
    dstate = grad_sum.value()
    for h in range(2):
        k_l = k_ref[:, head(2 + h)].astype(F32)
        v_l = v_ref[:, head(2 + h)]
        dk_lin = dot(v_l, dstate[h], 1, 1) * unit_slope(k_l)
        dk_ref[:, head(2 + h)] = dk_lin.astype(BF16)
        dv_ref[:, head(2 + h)] = dot_wide(unit_plus(k_l), dstate[h], 1, 0).astype(BF16)

    for step in steps:
        to_dp, flip, cross = step
        index = fin_base + flip * 8 + to_dp * 2 + cross
        pltpu.make_async_remote_copy(
            src_ref=wg_sum.at[0, 0],
            dst_ref=wg_fin.at[0, 0, 0],
            send_sem=ssem.at[index],
            recv_sem=rsem.at[index],
            device_id=column_peer(step),
            device_id_type=MESH,
        ).wait_recv()
    for c in range(2):
        for half in range(2):
            total = (wg_fin[0, c, half] + wg_fin[1, c, half]) + (wg_fin[2, c, half] + wg_fin[3, c, half])
            first = c * 512 + half * 256
            wg_ref[:, first : first + 256] = total * (1.0 / math.sqrt(N_DP * N_SEQ * ROWS))
    wg_soft.finish()
    wg_lin.finish()
    for copy in started:
        copy.wait_send()
    assert used[0] == N_COPIES, used[0]


N_COPIES = (
    2 * (15 + 7 + 15)
    + 15 + 7 + 8
    + 4 + 1 + 2
    + 2 * (7 + 7)
    + 2
)


def writer(dq, dk, dv, wg, dq_out, dk_out, dv_out, wg_out, sem):
    copies = [
        pltpu.make_async_copy(src, dst, sem.at[i])
        for i, (src, dst) in enumerate(((dq, dq_out), (dk, dk_out), (dv, dv_out), (wg, wg_out)))
    ]
    for copy in copies:
        copy.start()
    for copy in copies:
        copy.wait()


RESULTS = (((ROWS, 512), BF16), ((ROWS, 512), BF16), ((ROWS, 512), BF16), ((4, 1024), F32))


def body(queries, key_rows, value_rows, out_grad, out_weight, norm_gain):
    vmem = pl.BlockSpec(memory_space=pltpu.VMEM)
    hbm = pl.BlockSpec(memory_space=pltpu.HBM)
    out = pl.pallas_call(
        kernel,
        out_shape=tuple(pltpu.VMEM(*result) for result in RESULTS),
        in_specs=[hbm] * 6,
        out_specs=(vmem,) * 4,
        scratch_shapes=[
            pltpu.VMEM((ROWS, 512), BF16),
            pltpu.VMEM((ROWS, 512), BF16),
            pltpu.VMEM((ROWS, 512), BF16),
            pltpu.VMEM((ROWS, 1024), BF16),
            pltpu.VMEM((4, 1024), BF16),
            pltpu.VMEM((2, DH), F32),
            pltpu.VMEM((2, ROWS, SOFT), BF16),
            pltpu.VMEM((2, ROWS, SOFT), BF16),
            pltpu.VMEM((2, 2, ROWS, DH), BF16),
            pltpu.VMEM((2, 2, DH, ROWS), BF16),
            pltpu.VMEM((2, 2, 8, 16, DH), BF16),
            pltpu.VMEM((2, 8, 2, 16, DH), BF16),
            pltpu.VMEM((2, 8, 16, DH), BF16),
            pltpu.VMEM((2, 2, 8, 16, DH), BF16),
            pltpu.VMEM((16, 4, 512), BF16),
            pltpu.VMEM((64, 512), F32),
            pltpu.VMEM((2, 512, 512), BF16),
            pltpu.VMEM((ROWS, 512), BF16),
            pltpu.VMEM((ROWS, 512), BF16),
            pltpu.VMEM((ROWS, 512), BF16),
            pltpu.VMEM((2, 3, ROWS, ROWS), F32),
            pltpu.VMEM((2, ROWS, DH), F32),
            pltpu.VMEM((2, 8, 64, 256), BF16),
            pltpu.VMEM((2, 8, 64, 256), BF16),
            pltpu.VMEM((2, 8, 8, 256), BF16),
            pltpu.VMEM((2, 8, 8, 256), BF16),
            pltpu.VMEM((2, 2, 4, 256), F32),
            pltpu.VMEM((N_DP, 2, 2, 4, 256), F32),
            pltpu.VMEM((2, 2, ROWS, SOFT), BF16),
            pltpu.VMEM((2, 2, ROWS, SOFT), BF16),
            pltpu.VMEM((2, ROWS, SOFT), F32),
            pltpu.SemaphoreType.DMA((6,)),
            pltpu.SemaphoreType.DMA((N_COPIES + 16,)),
            pltpu.SemaphoreType.DMA((N_COPIES + 16,)),
        ],
        compiler_params=pltpu.CompilerParams(collective_id=0, has_side_effects=True),
        name="sublayer_backward",
    )(
        queries[0],
        key_rows[0],
        value_rows[0],
        out_grad[0],
        out_weight,
        norm_gain.reshape(2, DH),
    )
    out = pl.pallas_call(
        writer,
        out_shape=tuple(jax.ShapeDtypeStruct(*result) for result in RESULTS),
        in_specs=[vmem] * 4,
        out_specs=(hbm,) * 4,
        scratch_shapes=[pltpu.SemaphoreType.DMA((4,))],
        name="write_out",
    )(*[pltpu.with_memory_space_constraint(x, pltpu.VMEM) for x in out])
    return (out[0][None], out[1][None], out[2][None], out[3])


def solution(mesh):
    return jax.shard_map(
        body,
        mesh=mesh,
        in_specs=(
            P("dp", "seq", None),
            P("dp", "seq", None),
            P("dp", "seq", None),
            P("dp", "seq", None),
            P("seq", None),
            P(),
        ),
        out_specs=(
            P("dp", "seq", None),
            P("dp", "seq", None),
            P("dp", "seq", None),
            P("seq", None),
        ),
        check_vma=False,
    )
```

```python
import math

import jax
import jax.numpy as jnp
from jax import lax
from jax.experimental import pallas as pl
from jax.experimental.pallas import tpu as pltpu
from jax.sharding import PartitionSpec as P

MESH = pl.DeviceIdType.MESH
DH = 128
ROWS = 128
SOFT = 256
N_SEQ = 128
N_DP = 4
WIDE = 384
norm_eps = 1e-06
BF16 = jnp.bfloat16
F32 = jnp.float32
FAR = (4, 3, 5, 2, 6, 1, 7)


def dot(a, b, a_dim, b_dim):
    return lax.dot_general(a, b, (((a_dim,), (b_dim,)), ((), ())), preferred_element_type=F32)


def parts(x):
    high = x.astype(BF16)
    return high, (x - high.astype(F32)).astype(BF16)


def dot_wide(a, b, a_dim, b_dim):
    if b.dtype == BF16:
        high, low = parts(a)
        return dot(high, b, a_dim, b_dim) + dot(low, b, a_dim, b_dim)
    if a.dtype == BF16:
        high, low = parts(b)
        return dot(a, high, a_dim, b_dim) + dot(a, low, a_dim, b_dim)
    a_high, a_low = parts(a)
    b_high, b_low = parts(b)
    return (
        dot(a_high, b_high, a_dim, b_dim)
        + dot(a_high, b_low, a_dim, b_dim)
        + dot(a_low, b_high, a_dim, b_dim)
    )


def unit_plus(x):
    return jnp.where(x > 0, x + 1.0, jnp.exp(jnp.minimum(x, 0.0)))


def unit_slope(x):
    return jnp.where(x > 0, 1.0, jnp.exp(jnp.minimum(x, 0.0)))


def head(h):
    return slice(h * DH, (h + 1) * DH)


def kernel(
    q_hbm, k_hbm, v_hbm, g_hbm, w_hbm, gain_hbm,
    dq_ref, dk_ref, dv_ref, wg_ref,
    q_ref, k_ref, v_ref, g_ref, w_ref, gain_ref,
    kx, vx, phi_part, phi_turned, key_part, slope_keep, term, s_xy, s_z, s_full,
    w_in, w_rows, w_all, t_in, t_rows, t_all, t_sorted, g_in, attn_own, attn_in,
    probs, u_keep, wg_out, wg_in, wg_zout, wg_zin, wg_sum, wg_fin,
    back_out, back_in, dkv_keep,
    lsem, ssem, rsem,
):
    dp = lax.axis_index("dp")
    seq = lax.axis_index("seq")
    core = seq % 2
    z = (seq // 2) % 8
    p = seq // 16
    y = p // 4
    other = 1 - core
    partner = seq + 1 - 2 * core
    after = (seq + 1) % N_SEQ
    before = (seq + N_SEQ - 1) % N_SEQ
    factor = DH ** (-0.5)

    loads = [
        pltpu.make_async_copy(src, dst, lsem.at[i])
        for i, (src, dst) in enumerate(
            (
                (k_hbm.at[:, pl.ds(SOFT, SOFT)], k_ref.at[:, pl.ds(SOFT, SOFT)]),
                (v_hbm.at[:, pl.ds(SOFT, SOFT)], v_ref.at[:, pl.ds(SOFT, SOFT)]),
                (w_hbm, w_ref),
                (k_hbm.at[:, pl.ds(0, SOFT)], k_ref.at[:, pl.ds(0, SOFT)]),
                (v_hbm.at[:, pl.ds(0, SOFT)], v_ref.at[:, pl.ds(0, SOFT)]),
                (q_hbm, q_ref),
                (gain_hbm, gain_ref),
                (g_hbm, g_ref),
            )
        )
    ]
    for load in loads:
        load.start()

    def xy_peer(d):
        return (((p + d) % 8) * 8 + z) * 2 + core

    def flat_peer(d, cross):
        return (((p + d) % 8) * 8 + z) * 2 + (core + cross) % 2

    def z_peer(d):
        return (p * 8 + (z + d) % 8) * 2 + core

    def z_cross(d):
        return (p * 8 + (z + d) % 8) * 2 + other

    def column_peer(step):
        to_dp, flip, cross = step
        chip = ((p + 4 * flip) % 8) * 8 + z
        return (dp + to_dp) % N_DP, chip * 2 + (core + cross) % 2

    steps = [(a, b, c) for a in (2, 1, 3, 0) for b in range(2) for c in range(2)][:-4]
    steps += [(0, 1, 1), (0, 1, 0), (0, 0, 1)]

    barrier = pltpu.get_barrier_semaphore()
    peers = [column_peer(step) for step in steps]
    peers += [(dp, z_peer(d)) for d in FAR]
    peers += [(dp, z_cross(d)) for d in FAR]
    peers += [(dp, flat_peer(d, cross)) for d in FAR if d != 4 for cross in range(2)]
    peers += [(dp, after), (dp, before)]
    for peer in peers:
        pl.semaphore_signal(barrier, inc=1, device_id=peer, device_id_type=MESH)

    used = [0]
    started = []
    fin_base = N_COPIES

    def send(src, dst, device, dp_to=None):
        index = used[0]
        used[0] += 1
        copy = pltpu.make_async_remote_copy(
            src_ref=src,
            dst_ref=dst,
            send_sem=ssem.at[index],
            recv_sem=rsem.at[index],
            device_id=(dp if dp_to is None else dp_to, device),
            device_id_type=MESH,
        )
        copy.start()
        started.append(copy)
        return copy

    def arrived(copies):
        for copy in copies:
            copy.wait_recv()

    near = [(d, cross) for d in FAR for cross in range(2)] + [(0, 1)]

    class Total:
        def __init__(self, slot, terms):
            self.i = slot
            for h in range(2):
                term[slot, h] = terms[h].astype(BF16).reshape(8, 16, DH)

        def start(self):
            i = self.i
            self.c = [
                send(term.at[i, (core + cross) % 2, (p + d) % 8], s_xy.at[i, d, cross], flat_peer(d, cross))
                for d, cross in near
            ]

        def along_z(self):
            i = self.i
            arrived(self.c)
            total = term[i, core, p].astype(F32)
            for d, cross in near[::-1]:
                total = total + s_xy[i, d, cross].astype(F32)
            s_z[i, z] = total.astype(BF16)
            self.c = [send(s_z.at[i, z], s_z.at[i, z], z_peer(d)) for d in FAR]

        def spread(self):
            i = self.i
            arrived(self.c)
            total = s_z[i, 0].astype(F32)
            for d in range(1, 8):
                total = total + s_z[i, d].astype(F32)
            s_full[i, core, p] = total.astype(BF16)
            mine = s_full.at[i, core, p]
            self.c = [send(mine, mine, flat_peer(d, cross)) for d, cross in near]

        def value(self):
            arrived(self.c)
            return [s_full[self.i, h].reshape(DH, DH) for h in range(2)]

    class Half:
        def __init__(self, half, g_mine, g_other):
            self.s = s = half
            for b in range(4):
                rows = slice(s * SOFT + b * 64, s * SOFT + (b + 1) * 64)
                block = dot(attn_own[:, rows], g_mine, 0, 0) + dot(attn_in[:, rows], g_other, 0, 0)
                block = block.astype(BF16)
                wg_out[s, b] = block[:, 0:256]
                wg_out[s, 4 + b] = block[:, 256:512]

        def xy(self):
            s = self.s
            self.c = [send(wg_out.at[s, (p + d) % 8], wg_in.at[s, d], xy_peer(d)) for d in FAR]

        def along_z(self):
            s = self.s
            arrived(self.c)
            total = wg_out[s, p].astype(F32)
            for d in range(1, 8):
                total = total + wg_in[s, d].astype(F32)
            wg_zout[s] = total.reshape(8, 8, 256).astype(BF16)
            self.c = [send(wg_zout.at[s, (z + d) % 8], wg_zin.at[s, d], z_peer(d)) for d in FAR]

        def deliver(self):
            s = self.s
            arrived(self.c)
            total = wg_zout[s, z].astype(F32)
            for d in range(1, 8):
                total = total + wg_zin[s, d].astype(F32)
            for c in range(2):
                wg_sum[s, c] = total[4 * c : 4 * c + 4]
            flip = (s + y) % 2
            owner = ((s * 4 + p % 4) * 8 + z) * 2

            def copy_to(to_dp, cross):
                index = fin_base + flip * 8 + to_dp * 2 + cross
                core_to = (core + cross) % 2
                return pltpu.make_async_remote_copy(
                    src_ref=wg_sum.at[s, core_to],
                    dst_ref=wg_fin.at[dp, core, y],
                    send_sem=ssem.at[index],
                    recv_sem=rsem.at[index],
                    device_id=((dp + to_dp) % N_DP, owner + core_to),
                    device_id_type=MESH,
                )

            self.out = [copy_to(a, c) for a in (2, 1, 3) for c in range(2)] + [copy_to(0, 1)]
            for copy in self.out:
                copy.start()
            self.last = copy_to(0, 0)

            @pl.when(flip == 1)
            def _():
                self.last.start()

            @pl.when(flip == 0)
            def _():
                wg_fin[dp, core, y] = wg_sum[s, core]

        def finish(self):
            for copy in self.out:
                copy.wait_send()

            @pl.when((self.s + y) % 2 == 1)
            def _():
                self.last.wait_send()

    loads[0].wait()
    loads[1].wait()
    state_sum = Total(
        0,
        [
            dot(unit_plus(k_ref[:, head(2 + h)].astype(F32)).astype(BF16), v_ref[:, head(2 + h)], 0, 0)
            for h in range(2)
        ],
    )
    loads[2].wait()
    w_piece = jnp.where(core == 0, w_ref[:, 0:512].astype(F32), w_ref[:, 512:1024].astype(F32)).astype(BF16)
    w_in[z * 2 + core] = w_piece[:, 0:WIDE]
    t_in[p * 2 + core] = w_piece[:, WIDE:512]

    pl.semaphore_wait(barrier, len(peers))

    state_sum.start()
    def w_part(of, first, width):
        return w_hbm.at[:, pl.ds(pl.multiple_of(of * 512 + first, 128), width)]

    w_slot = w_in.at[z * 2 + core]
    w_copy = [send(w_part(other, 0, WIDE), w_slot, partner)]
    for d in FAR:
        w_copy.append(send(w_part(core, 0, WIDE), w_slot, z_peer(d)))
        w_copy.append(send(w_part(other, 0, WIDE), w_slot, z_cross(d)))
    t_slot = t_in.at[p * 2 + core]
    t_copy = [send(w_part((core + cross) % 2, WIDE, 128), t_slot, flat_peer(d, cross)) for d, cross in near]
    soft = pl.ds(0, SOFT)
    k_copy = [
        send(k_hbm.at[:, soft], kx.at[0], after),
        send(k_hbm.at[:, soft], kx.at[1], before),
    ]
    v_copy = [
        send(v_hbm.at[:, soft], vx.at[0], after),
        send(v_hbm.at[:, soft], vx.at[1], before),
    ]
    g_copy = [
        send(g_hbm.at[:, pl.ds(pl.multiple_of(other * 512, 512), 512)], g_in, partner)
    ]
    for load in loads[3:]:
        load.wait()

    for h in range(2):
        for i, part in enumerate(parts(unit_plus(q_ref[:, head(2 + h)].astype(F32)))):
            phi_part[h, i] = part
            if i == 0:
                phi_turned[h] = part.T
        k_l = k_ref[:, head(2 + h)].astype(F32)
        slope_keep[h] = unit_slope(k_l)
        for i, part in enumerate(parts(unit_plus(k_l))):
            key_part[h, i] = part

    state_sum.along_z()

    arrived(t_copy)
    for i in range(16):
        t_rows[4 * i : 4 * i + 4, :] = t_in[i].astype(F32)
    t_all[core, z] = t_rows[...].astype(BF16)
    t_mine = t_all.at[core, z]
    t_copy = [send(t_mine, t_mine, z_peer(d)) for d in FAR]

    arrived(w_copy)
    for i in range(16):
        w_rows[4 * i : 4 * i + 4, :] = w_in[i].astype(F32)

    def w_block(source):
        return w_all.at[core, pl.ds(pl.multiple_of(source * 64, 64), 64), :]

    w_all[core, pl.ds(pl.multiple_of(p * 64, 64), 64), :] = w_rows[...].astype(BF16)
    w_copy = {d: send(w_block(p), w_block(p), xy_peer(d)) for d in FAR}
    w_swap = [send(w_block(p), w_block(p), partner)]

    row_pos = lax.broadcasted_iota(jnp.int32, (ROWS, ROWS), 0)
    col_pos = lax.broadcasted_iota(jnp.int32, (ROWS, ROWS), 1)
    keep = (col_pos >= row_pos, None, col_pos < row_pos)
    arrived(k_copy)

    def span_of(halo, ref, h):
        return (halo[0, :, head(h)], ref[:, head(h)], halo[1, :, head(h)])

    for h in range(2):
        k_span = span_of(kx, k_ref, h)
        q_h = q_ref[:, head(h)]
        scores = []
        for b in range(3):
            s = dot(q_h, k_span[b], 1, 1) * factor
            scores.append(s if keep[b] is None else jnp.where(keep[b], s, -1e30))
        peak = jnp.max(jnp.maximum(jnp.maximum(scores[0], scores[1]), scores[2]), axis=1, keepdims=True)
        terms = []
        for b in range(3):
            e = jnp.exp(scores[b] - peak)
            terms.append(e if keep[b] is None else jnp.where(keep[b], e, 0.0))
        whole = jnp.sum(terms[0] + terms[1] + terms[2], axis=1, keepdims=True)
        for b in range(3):
            probs[h, b] = terms[b] / whole

    arrived(v_copy)
    for h in range(2):
        v_span = span_of(vx, v_ref, h)
        total = dot(probs[h, 0].astype(BF16), v_span[0], 1, 0)
        for b in range(1, 3):
            total = total + dot(probs[h, b].astype(BF16), v_span[b], 1, 0)
        attn_own[:, head(h)] = total.astype(BF16)
    a_copy = [send(attn_own.at[:, soft], attn_in.at[:, soft], partner)]

    state_sum.spread()

    arrived(g_copy)
    arrived(a_copy)
    g_mine = g_ref[:, pl.ds(pl.multiple_of(core * 512, 512), 512)]
    wg_soft = Half(0, g_mine, g_in[...])
    wg_soft.xy()

    for d in FAR[::-1]:
        w_copy[d].wait_recv()
        block = w_block((p + 8 - d) % 8)
        w_swap.append(send(block, block, partner))
    arrived(t_copy)
    w_swap.append(send(t_all.at[core], t_all.at[core], partner))

    def t_sort(c, groups):
        for group in groups:
            for i in range(8):
                first = group * 64 + i * 8
                t_sorted[c, first : first + 8, :] = t_all[c, i, group * 8 : group * 8 + 8, :]

    def d_attn_of(c, rows):
        wide = dot(g_ref[:, c * 512 : c * 512 + WIDE], w_all[c, rows, :], 1, 1)
        return wide + dot(g_ref[:, c * 512 + WIDE : c * 512 + 512], t_sorted[c, rows, :], 1, 1)

    state = state_sum.value()

    lin_r = []
    for h in range(2):
        u = dot(phi_part[h, 0], state[h], 1, 0) + dot(phi_part[h, 1], state[h], 1, 0)
        r = lax.rsqrt(jnp.mean(u * u, axis=1, keepdims=True) + norm_eps)
        u_keep[h] = u
        lin_r.append(r)
        attn_own[:, head(2 + h)] = (gain_ref[h : h + 1, :] * u * r).astype(BF16)
    lin = pl.ds(SOFT, SOFT)
    a_copy = [send(attn_own.at[:, lin], attn_in.at[:, lin], partner)]

    arrived(w_swap)
    for c in range(2):
        t_sort(c, range(4, 8))
    d_attn_lin = (d_attn_of(0, slice(SOFT, 512)) + d_attn_of(1, slice(SOFT, 512))).astype(BF16)

    grad_u = []
    for h in range(2):
        g_lin = gain_ref[h : h + 1, :] * d_attn_lin[:, head(h)].astype(F32)
        u = u_keep[h]
        r = lin_r[h]
        grad_u.append(r * g_lin - u * (r * r * r) * jnp.mean(g_lin * u, axis=1, keepdims=True))
    terms = []
    for h in range(2):
        terms.append(dot(phi_turned[h], grad_u[h].astype(BF16), 1, 0))
    grad_sum = Total(1, terms)
    grad_sum.start()

    arrived(a_copy)
    wg_lin = Half(1, g_mine, g_in[...])
    wg_lin.xy()
    for c in range(2):
        t_sort(c, range(4))
    d_attn = (d_attn_of(0, slice(0, SOFT)) + d_attn_of(1, slice(0, SOFT))).astype(BF16)
    wg_soft.along_z()

    for h in range(2):
        k_span = span_of(kx, k_ref, h)
        v_span = span_of(vx, v_ref, h)
        q_h = q_ref[:, head(h)]
        da = d_attn[:, head(h)]
        delta = jnp.sum(da.astype(F32) * attn_own[:, head(h)].astype(F32), axis=1, keepdims=True)
        dq = None
        for b in range(3):
            pr = probs[h, b]
            ds = (pr * (dot(da, v_span[b], 1, 1) - delta)).astype(BF16)
            step = dot(ds, k_span[b], 1, 0)
            dq = step if dq is None else dq + step
            dk = dot(ds, q_h, 0, 0) * factor
            dv = dot(pr.astype(BF16), da, 0, 0)
            if b == 1:
                dkv_keep[0, :, head(h)] = dk
                dkv_keep[1, :, head(h)] = dv
            else:
                back_out[b // 2, 0, :, head(h)] = dk.astype(BF16)
                back_out[b // 2, 1, :, head(h)] = dv.astype(BF16)
        dq_ref[:, head(h)] = (dq * factor).astype(BF16)
    grad_sum.along_z()

    back_copy = [
        send(back_out.at[0], back_in.at[0], before),
        send(back_out.at[1], back_in.at[1], after),
    ]

    for h in range(2):
        q_lin = q_ref[:, head(2 + h)].astype(F32)
        dq_lin = dot_wide(grad_u[h], state[h], 1, 1) * unit_slope(q_lin)
        dq_ref[:, head(2 + h)] = dq_lin.astype(BF16)

    wg_lin.along_z()
    wg_soft.deliver()
    grad_sum.spread()

    arrived(back_copy)
    for h in range(2):
        for t, out in ((0, dk_ref), (1, dv_ref)):
            total = dkv_keep[t, :, head(h)] + back_in[1, t, :, head(h)].astype(F32)
            total = total + back_in[0, t, :, head(h)].astype(F32)
            out[:, head(h)] = total.astype(BF16)

    wg_lin.deliver()
    dstate = grad_sum.value()
    for h in range(2):
        dk_lin = dot(v_ref[:, head(2 + h)], dstate[h], 1, 1) * slope_keep[h]
        dk_ref[:, head(2 + h)] = dk_lin.astype(BF16)
        dv_lin = dot(key_part[h, 0], dstate[h], 1, 0) + dot(key_part[h, 1], dstate[h], 1, 0)
        dv_ref[:, head(2 + h)] = dv_lin.astype(BF16)

    for step in steps:
        to_dp, flip, cross = step
        index = fin_base + flip * 8 + to_dp * 2 + cross
        pltpu.make_async_remote_copy(
            src_ref=wg_sum.at[0, 0],
            dst_ref=wg_fin.at[0, 0, 0],
            send_sem=ssem.at[index],
            recv_sem=rsem.at[index],
            device_id=column_peer(step),
            device_id_type=MESH,
        ).wait_recv()
    for c in range(2):
        for half in range(2):
            total = (wg_fin[0, c, half] + wg_fin[1, c, half]) + (wg_fin[2, c, half] + wg_fin[3, c, half])
            first = c * 512 + half * 256
            wg_ref[:, first : first + 256] = total * (1.0 / math.sqrt(N_DP * N_SEQ * ROWS))
    wg_soft.finish()
    wg_lin.finish()
    for copy in started:
        copy.wait_send()
    assert used[0] == N_COPIES, used[0]


N_COPIES = (
    2 * (15 + 7 + 15)
    + 15 + 7 + 8 + 15 + 7 + 1
    + 4 + 1 + 2
    + 2 * (7 + 7)
    + 2
)


def writer(dq, dk, dv, wg, dq_out, dk_out, dv_out, wg_out, sem):
    copies = [
        pltpu.make_async_copy(src, dst, sem.at[i])
        for i, (src, dst) in enumerate(((dq, dq_out), (dk, dk_out), (dv, dv_out), (wg, wg_out)))
    ]
    for copy in copies:
        copy.start()
    for copy in copies:
        copy.wait()


RESULTS = (((ROWS, 512), BF16), ((ROWS, 512), BF16), ((ROWS, 512), BF16), ((4, 1024), F32))


def body(queries, key_rows, value_rows, out_grad, out_weight, norm_gain):
    vmem = pl.BlockSpec(memory_space=pltpu.VMEM)
    hbm = pl.BlockSpec(memory_space=pltpu.HBM)
    out = pl.pallas_call(
        kernel,
        out_shape=tuple(pltpu.VMEM(*result) for result in RESULTS),
        in_specs=[hbm] * 6,
        out_specs=(vmem,) * 4,
        scratch_shapes=[
            pltpu.VMEM((ROWS, 512), BF16),
            pltpu.VMEM((ROWS, 512), BF16),
            pltpu.VMEM((ROWS, 512), BF16),
            pltpu.VMEM((ROWS, 1024), BF16),
            pltpu.VMEM((4, 1024), BF16),
            pltpu.VMEM((2, DH), F32),
            pltpu.VMEM((2, ROWS, SOFT), BF16),
            pltpu.VMEM((2, ROWS, SOFT), BF16),
            pltpu.VMEM((2, 2, ROWS, DH), BF16),
            pltpu.VMEM((2, DH, ROWS), BF16),
            pltpu.VMEM((2, 2, ROWS, DH), BF16),
            pltpu.VMEM((2, ROWS, DH), F32),
            pltpu.VMEM((2, 2, 8, 16, DH), BF16),
            pltpu.VMEM((2, 8, 2, 16, DH), BF16),
            pltpu.VMEM((2, 8, 16, DH), BF16),
            pltpu.VMEM((2, 2, 8, 16, DH), BF16),
            pltpu.VMEM((16, 4, WIDE), BF16),
            pltpu.VMEM((64, WIDE), F32),
            pltpu.VMEM((2, 512, WIDE), BF16),
            pltpu.VMEM((16, 4, 128), BF16),
            pltpu.VMEM((64, 128), F32),
            pltpu.VMEM((2, 8, 64, 128), BF16),
            pltpu.VMEM((2, 512, 128), BF16),
            pltpu.VMEM((ROWS, 512), BF16),
            pltpu.VMEM((ROWS, 512), BF16),
            pltpu.VMEM((ROWS, 512), BF16),
            pltpu.VMEM((2, 3, ROWS, ROWS), F32),
            pltpu.VMEM((2, ROWS, DH), F32),
            pltpu.VMEM((2, 8, 64, 256), BF16),
            pltpu.VMEM((2, 8, 64, 256), BF16),
            pltpu.VMEM((2, 8, 8, 256), BF16),
            pltpu.VMEM((2, 8, 8, 256), BF16),
            pltpu.VMEM((2, 2, 4, 256), F32),
            pltpu.VMEM((N_DP, 2, 2, 4, 256), F32),
            pltpu.VMEM((2, 2, ROWS, SOFT), BF16),
            pltpu.VMEM((2, 2, ROWS, SOFT), BF16),
            pltpu.VMEM((2, ROWS, SOFT), F32),
            pltpu.SemaphoreType.DMA((8,)),
            pltpu.SemaphoreType.DMA((N_COPIES + 16,)),
            pltpu.SemaphoreType.DMA((N_COPIES + 16,)),
        ],
        compiler_params=pltpu.CompilerParams(collective_id=0, has_side_effects=True),
        name="sublayer_backward",
    )(
        queries[0],
        key_rows[0],
        value_rows[0],
        out_grad[0],
        out_weight,
        norm_gain.reshape(2, DH),
    )
    out = pl.pallas_call(
        writer,
        out_shape=tuple(jax.ShapeDtypeStruct(*result) for result in RESULTS),
        in_specs=[vmem] * 4,
        out_specs=(hbm,) * 4,
        scratch_shapes=[pltpu.SemaphoreType.DMA((4,))],
        name="write_out",
    )(*[pltpu.with_memory_space_constraint(x, pltpu.VMEM) for x in out])
    return (out[0][None], out[1][None], out[2][None], out[3])


def solution(mesh):
    return jax.shard_map(
        body,
        mesh=mesh,
        in_specs=(
            P("dp", "seq", None),
            P("dp", "seq", None),
            P("dp", "seq", None),
            P("dp", "seq", None),
            P("seq", None),
            P(),
        ),
        out_specs=(
            P("dp", "seq", None),
            P("dp", "seq", None),
            P("dp", "seq", None),
            P("seq", None),
        ),
        check_vma=False,
    )
```

```python
import math

import jax
import jax.numpy as jnp
from jax import lax
from jax.experimental import pallas as pl
from jax.experimental.pallas import tpu as pltpu
from jax.sharding import PartitionSpec as P

MESH = pl.DeviceIdType.MESH
DH = 128
ROWS = 128
SOFT = 256
N_SEQ = 128
N_DP = 4
WIDE = 384
norm_eps = 1e-06
BF16 = jnp.bfloat16
F32 = jnp.float32
FAR = (4, 3, 5, 2, 6, 1, 7)


def dot(a, b, a_dim, b_dim):
    return lax.dot_general(a, b, (((a_dim,), (b_dim,)), ((), ())), preferred_element_type=F32)


def parts(x):
    high = x.astype(BF16)
    return high, (x - high.astype(F32)).astype(BF16)


def dot_wide(a, b, a_dim, b_dim):
    if b.dtype == BF16:
        high, low = parts(a)
        return dot(high, b, a_dim, b_dim) + dot(low, b, a_dim, b_dim)
    if a.dtype == BF16:
        high, low = parts(b)
        return dot(a, high, a_dim, b_dim) + dot(a, low, a_dim, b_dim)
    a_high, a_low = parts(a)
    b_high, b_low = parts(b)
    return (
        dot(a_high, b_high, a_dim, b_dim)
        + dot(a_high, b_low, a_dim, b_dim)
        + dot(a_low, b_high, a_dim, b_dim)
    )


def unit_plus(x):
    return jnp.where(x > 0, x + 1.0, jnp.exp(jnp.minimum(x, 0.0)))


def unit_slope(x):
    return jnp.where(x > 0, 1.0, jnp.exp(jnp.minimum(x, 0.0)))


def head(h):
    return slice(h * DH, (h + 1) * DH)


def kernel(
    q_hbm, k_hbm, v_hbm, g_hbm, w_hbm, gain_hbm,
    dq_ref, dk_ref, dv_ref, wg_ref,
    q_ref, k_ref, v_ref, g_ref, w_ref, gain_ref,
    kx, vx, phi_part, phi_turned, key_part, slope_keep, term, s_xy, s_z, s_full,
    w_in, w_rows, w_all, t_in, t_rows, t_all, t_sorted, g_in, attn_own, attn_in,
    probs, u_keep, wg_out, wg_in, wg_zout, wg_zin, wg_sum, wg_fin,
    back_out, back_in, dkv_keep,
    lsem, ssem, rsem,
):
    dp = lax.axis_index("dp")
    seq = lax.axis_index("seq")
    core = seq % 2
    z = (seq // 2) % 8
    p = seq // 16
    y = p // 4
    other = 1 - core
    partner = seq + 1 - 2 * core
    after = (seq + 1) % N_SEQ
    before = (seq + N_SEQ - 1) % N_SEQ
    factor = DH ** (-0.5)

    loads = [
        pltpu.make_async_copy(src, dst, lsem.at[i])
        for i, (src, dst) in enumerate(
            (
                (k_hbm.at[:, pl.ds(SOFT, SOFT)], k_ref.at[:, pl.ds(SOFT, SOFT)]),
                (v_hbm.at[:, pl.ds(SOFT, SOFT)], v_ref.at[:, pl.ds(SOFT, SOFT)]),
                (w_hbm, w_ref),
                (k_hbm.at[:, pl.ds(0, SOFT)], k_ref.at[:, pl.ds(0, SOFT)]),
                (v_hbm.at[:, pl.ds(0, SOFT)], v_ref.at[:, pl.ds(0, SOFT)]),
                (q_hbm, q_ref),
                (gain_hbm, gain_ref),
                (g_hbm, g_ref),
            )
        )
    ]
    for load in loads:
        load.start()

    def xy_peer(d):
        return (((p + d) % 8) * 8 + z) * 2 + core

    def flat_peer(d, cross):
        return (((p + d) % 8) * 8 + z) * 2 + (core + cross) % 2

    def z_peer(d):
        return (p * 8 + (z + d) % 8) * 2 + core

    def z_cross(d):
        return (p * 8 + (z + d) % 8) * 2 + other

    def column_peer(step):
        to_dp, flip, cross = step
        chip = ((p + 4 * flip) % 8) * 8 + z
        return (dp + to_dp) % N_DP, chip * 2 + (core + cross) % 2

    steps = [(a, b, c) for a in (2, 1, 3, 0) for b in range(2) for c in range(2)][:-4]
    steps += [(0, 1, 1), (0, 1, 0), (0, 0, 1)]

    barrier = pltpu.get_barrier_semaphore()
    peers = [column_peer(step) for step in steps]
    peers += [(dp, z_peer(d)) for d in FAR]
    peers += [(dp, z_cross(d)) for d in FAR]
    peers += [(dp, flat_peer(d, cross)) for d in FAR if d != 4 for cross in range(2)]
    peers += [(dp, after), (dp, before)]
    for peer in peers:
        pl.semaphore_signal(barrier, inc=1, device_id=peer, device_id_type=MESH)

    used = [0]
    started = []
    fin_base = N_COPIES

    def send(src, dst, device, dp_to=None):
        index = used[0]
        used[0] += 1
        copy = pltpu.make_async_remote_copy(
            src_ref=src,
            dst_ref=dst,
            send_sem=ssem.at[index],
            recv_sem=rsem.at[index],
            device_id=(dp if dp_to is None else dp_to, device),
            device_id_type=MESH,
        )
        copy.start()
        started.append(copy)
        return copy

    def arrived(copies):
        for copy in copies:
            copy.wait_recv()

    near = [(d, cross) for d in FAR for cross in range(2)] + [(0, 1)]

    class Total:
        def __init__(self, slot, terms):
            self.i = slot
            for h in range(2):
                term[slot, h] = terms[h].astype(BF16).reshape(8, 16, DH)

        def start(self):
            i = self.i
            self.c = [
                send(term.at[i, (core + cross) % 2, (p + d) % 8], s_xy.at[i, d, cross], flat_peer(d, cross))
                for d, cross in near
            ]

        def along_z(self):
            i = self.i
            arrived(self.c)
            total = term[i, core, p].astype(F32)
            for d, cross in near[::-1]:
                total = total + s_xy[i, d, cross].astype(F32)
            s_z[i, z] = total.astype(BF16)
            self.c = [send(s_z.at[i, z], s_z.at[i, z], z_peer(d)) for d in FAR]

        def spread(self):
            i = self.i
            arrived(self.c)
            total = s_z[i, 0].astype(F32)
            for d in range(1, 8):
                total = total + s_z[i, d].astype(F32)
            s_full[i, core, p] = total.astype(BF16)
            mine = s_full.at[i, core, p]
            self.c = [send(mine, mine, flat_peer(d, cross)) for d, cross in near]

        def value(self):
            arrived(self.c)
            return [s_full[self.i, h].reshape(DH, DH) for h in range(2)]

    class Half:
        def __init__(self, half, g_mine):
            self.s = s = half
            self.own = [dot(attn_own[:, self.rows(b)], g_mine, 0, 0) for b in range(4)]

        def rows(self, b):
            return slice(self.s * SOFT + b * 64, self.s * SOFT + (b + 1) * 64)

        def join(self, g_other):
            s = self.s
            for b in range(4):
                block = (self.own[b] + dot(attn_in[:, self.rows(b)], g_other, 0, 0)).astype(BF16)
                wg_out[s, b] = block[:, 0:256]
                wg_out[s, 4 + b] = block[:, 256:512]

        def xy(self):
            s = self.s
            self.c = [send(wg_out.at[s, (p + d) % 8], wg_in.at[s, d], xy_peer(d)) for d in FAR]

        def along_z(self):
            s = self.s
            arrived(self.c)
            total = wg_out[s, p].astype(F32)
            for d in range(1, 8):
                total = total + wg_in[s, d].astype(F32)
            wg_zout[s] = total.reshape(8, 8, 256).astype(BF16)
            self.c = [send(wg_zout.at[s, (z + d) % 8], wg_zin.at[s, d], z_peer(d)) for d in FAR]

        def deliver(self):
            s = self.s
            arrived(self.c)
            total = wg_zout[s, z].astype(F32)
            for d in range(1, 8):
                total = total + wg_zin[s, d].astype(F32)
            for c in range(2):
                wg_sum[s, c] = total[4 * c : 4 * c + 4].astype(BF16)
            flip = (s + y) % 2
            owner = ((s * 4 + p % 4) * 8 + z) * 2

            def copy_to(to_dp, cross):
                index = fin_base + flip * 8 + to_dp * 2 + cross
                core_to = (core + cross) % 2
                return pltpu.make_async_remote_copy(
                    src_ref=wg_sum.at[s, core_to],
                    dst_ref=wg_fin.at[dp, core, y],
                    send_sem=ssem.at[index],
                    recv_sem=rsem.at[index],
                    device_id=((dp + to_dp) % N_DP, owner + core_to),
                    device_id_type=MESH,
                )

            self.out = [copy_to(a, c) for a in (2, 1, 3) for c in range(2)] + [copy_to(0, 1)]
            for copy in self.out:
                copy.start()
            self.last = copy_to(0, 0)

            @pl.when(flip == 1)
            def _():
                self.last.start()

            @pl.when(flip == 0)
            def _():
                wg_fin[dp, core, y] = wg_sum[s, core]

        def finish(self):
            for copy in self.out:
                copy.wait_send()

            @pl.when((self.s + y) % 2 == 1)
            def _():
                self.last.wait_send()

    loads[0].wait()
    loads[1].wait()
    state_sum = Total(
        0,
        [
            dot(unit_plus(k_ref[:, head(2 + h)].astype(F32)).astype(BF16), v_ref[:, head(2 + h)], 0, 0)
            for h in range(2)
        ],
    )
    loads[2].wait()
    w_piece = jnp.where(core == 0, w_ref[:, 0:512].astype(F32), w_ref[:, 512:1024].astype(F32)).astype(BF16)
    w_in[z * 2 + core] = w_piece[:, 0:WIDE]
    t_in[p * 2 + core] = w_piece[:, WIDE:512]

    pl.semaphore_wait(barrier, len(peers))

    state_sum.start()
    def w_part(of, first, width):
        return w_hbm.at[:, pl.ds(pl.multiple_of(of * 512 + first, 128), width)]

    w_slot = w_in.at[z * 2 + core]
    w_copy = [send(w_part(other, 0, WIDE), w_slot, partner)]
    for d in FAR:
        w_copy.append(send(w_part(core, 0, WIDE), w_slot, z_peer(d)))
        w_copy.append(send(w_part(other, 0, WIDE), w_slot, z_cross(d)))
    t_slot = t_in.at[p * 2 + core]
    t_copy = [send(w_part((core + cross) % 2, WIDE, 128), t_slot, flat_peer(d, cross)) for d, cross in near]
    soft = pl.ds(0, SOFT)
    k_copy = [
        send(k_hbm.at[:, soft], kx.at[0], after),
        send(k_hbm.at[:, soft], kx.at[1], before),
    ]
    v_copy = [
        send(v_hbm.at[:, soft], vx.at[0], after),
        send(v_hbm.at[:, soft], vx.at[1], before),
    ]
    g_copy = [
        send(g_hbm.at[:, pl.ds(pl.multiple_of(other * 512, 512), 512)], g_in, partner)
    ]
    for load in loads[3:]:
        load.wait()

    for h in range(2):
        for i, part in enumerate(parts(unit_plus(q_ref[:, head(2 + h)].astype(F32)))):
            phi_part[h, i] = part
            if i == 0:
                phi_turned[h] = part.T
        k_l = k_ref[:, head(2 + h)].astype(F32)
        slope_keep[h] = unit_slope(k_l)
        for i, part in enumerate(parts(unit_plus(k_l))):
            key_part[h, i] = part

    state_sum.along_z()

    arrived(t_copy)
    for i in range(16):
        t_rows[4 * i : 4 * i + 4, :] = t_in[i].astype(F32)
    t_all[core, z] = t_rows[...].astype(BF16)
    t_mine = t_all.at[core, z]
    t_copy = [send(t_mine, t_mine, z_peer(d)) for d in FAR]

    arrived(w_copy)
    for i in range(16):
        w_rows[4 * i : 4 * i + 4, :] = w_in[i].astype(F32)

    def w_block(source):
        return w_all.at[core, pl.ds(pl.multiple_of(source * 64, 64), 64), :]

    w_all[core, pl.ds(pl.multiple_of(p * 64, 64), 64), :] = w_rows[...].astype(BF16)
    w_copy = {d: send(w_block(p), w_block(p), xy_peer(d)) for d in FAR}
    w_swap = [send(w_block(p), w_block(p), partner)]

    row_pos = lax.broadcasted_iota(jnp.int32, (ROWS, ROWS), 0)
    col_pos = lax.broadcasted_iota(jnp.int32, (ROWS, ROWS), 1)
    keep = (col_pos >= row_pos, None, col_pos < row_pos)
    arrived(k_copy)

    def span_of(halo, ref, h):
        return (halo[0, :, head(h)], ref[:, head(h)], halo[1, :, head(h)])

    for h in range(2):
        k_span = span_of(kx, k_ref, h)
        q_h = q_ref[:, head(h)]
        scores = []
        for b in range(3):
            s = dot(q_h, k_span[b], 1, 1) * factor
            scores.append(s if keep[b] is None else jnp.where(keep[b], s, -1e30))
        peak = jnp.max(jnp.maximum(jnp.maximum(scores[0], scores[1]), scores[2]), axis=1, keepdims=True)
        terms = []
        for b in range(3):
            e = jnp.exp(scores[b] - peak)
            terms.append(e if keep[b] is None else jnp.where(keep[b], e, 0.0))
        whole = jnp.sum(terms[0] + terms[1] + terms[2], axis=1, keepdims=True)
        for b in range(3):
            probs[h, b] = terms[b] / whole

    arrived(v_copy)
    for h in range(2):
        v_span = span_of(vx, v_ref, h)
        total = dot(probs[h, 0].astype(BF16), v_span[0], 1, 0)
        for b in range(1, 3):
            total = total + dot(probs[h, b].astype(BF16), v_span[b], 1, 0)
        attn_own[:, head(h)] = total.astype(BF16)
    a_copy = [send(attn_own.at[:, soft], attn_in.at[:, soft], partner)]

    state_sum.spread()

    g_mine = g_ref[:, pl.ds(pl.multiple_of(core * 512, 512), 512)]
    wg_soft = Half(0, g_mine)
    arrived(g_copy)
    arrived(a_copy)
    wg_soft.join(g_in[...])
    wg_soft.xy()

    for d in FAR[::-1]:
        w_copy[d].wait_recv()
        block = w_block((p + 8 - d) % 8)
        w_swap.append(send(block, block, partner))
    arrived(t_copy)
    w_swap.append(send(t_all.at[core], t_all.at[core], partner))

    def t_sort(c, groups):
        for group in groups:
            for i in range(8):
                first = group * 64 + i * 8
                t_sorted[c, first : first + 8, :] = t_all[c, i, group * 8 : group * 8 + 8, :]

    def d_attn_of(c, rows):
        g_wide = g_ref[:, pl.ds(pl.multiple_of(c * 512, 128), WIDE)]
        g_rest = g_ref[:, pl.ds(pl.multiple_of(c * 512 + WIDE, 128), 128)]
        return dot(g_wide, w_all[c, rows, :], 1, 1) + dot(g_rest, t_sorted[c, rows, :], 1, 1)

    t_sort(core, range(4, 8))
    mine_lin = d_attn_of(core, slice(SOFT, 512))

    state = state_sum.value()

    lin_r = []
    for h in range(2):
        u = dot(phi_part[h, 0], state[h], 1, 0) + dot(phi_part[h, 1], state[h], 1, 0)
        r = lax.rsqrt(jnp.mean(u * u, axis=1, keepdims=True) + norm_eps)
        u_keep[h] = u
        lin_r.append(r)
        attn_own[:, head(2 + h)] = (gain_ref[h : h + 1, :] * u * r).astype(BF16)
    lin = pl.ds(SOFT, SOFT)
    a_copy = [send(attn_own.at[:, lin], attn_in.at[:, lin], partner)]

    arrived(w_swap)
    t_sort(other, range(4, 8))
    d_attn_lin = (mine_lin + d_attn_of(other, slice(SOFT, 512))).astype(BF16)

    grad_u = []
    for h in range(2):
        g_lin = gain_ref[h : h + 1, :] * d_attn_lin[:, head(h)].astype(F32)
        u = u_keep[h]
        r = lin_r[h]
        grad_u.append(r * g_lin - u * (r * r * r) * jnp.mean(g_lin * u, axis=1, keepdims=True))
    terms = []
    for h in range(2):
        terms.append(dot(phi_turned[h], grad_u[h].astype(BF16), 1, 0))
    grad_sum = Total(1, terms)
    grad_sum.start()
    wg_lin = Half(1, g_mine)
    arrived(a_copy)
    wg_lin.join(g_in[...])
    wg_lin.xy()

    for c in range(2):
        t_sort(c, range(4))
    d_attn = (d_attn_of(0, slice(0, SOFT)) + d_attn_of(1, slice(0, SOFT))).astype(BF16)
    wg_soft.along_z()

    for h in range(2):
        k_span = span_of(kx, k_ref, h)
        v_span = span_of(vx, v_ref, h)
        q_h = q_ref[:, head(h)]
        da = d_attn[:, head(h)]
        delta = jnp.sum(da.astype(F32) * attn_own[:, head(h)].astype(F32), axis=1, keepdims=True)
        dq = None
        for b in range(3):
            pr = probs[h, b]
            ds = (pr * (dot(da, v_span[b], 1, 1) - delta)).astype(BF16)
            step = dot(ds, k_span[b], 1, 0)
            dq = step if dq is None else dq + step
            dk = dot(ds, q_h, 0, 0) * factor
            dv = dot(pr.astype(BF16), da, 0, 0)
            if b == 1:
                dkv_keep[0, :, head(h)] = dk
                dkv_keep[1, :, head(h)] = dv
            else:
                back_out[b // 2, 0, :, head(h)] = dk.astype(BF16)
                back_out[b // 2, 1, :, head(h)] = dv.astype(BF16)
        dq_ref[:, head(h)] = (dq * factor).astype(BF16)
    grad_sum.along_z()

    back_copy = [
        send(back_out.at[0], back_in.at[0], before),
        send(back_out.at[1], back_in.at[1], after),
    ]

    for h in range(2):
        q_lin = q_ref[:, head(2 + h)].astype(F32)
        dq_lin = dot_wide(grad_u[h], state[h], 1, 1) * unit_slope(q_lin)
        dq_ref[:, head(2 + h)] = dq_lin.astype(BF16)

    wg_lin.along_z()
    wg_soft.deliver()
    grad_sum.spread()

    arrived(back_copy)
    for h in range(2):
        for t, out in ((0, dk_ref), (1, dv_ref)):
            total = dkv_keep[t, :, head(h)] + back_in[1, t, :, head(h)].astype(F32)
            total = total + back_in[0, t, :, head(h)].astype(F32)
            out[:, head(h)] = total.astype(BF16)

    wg_lin.deliver()
    dstate = grad_sum.value()
    for h in range(2):
        dk_lin = dot(v_ref[:, head(2 + h)], dstate[h], 1, 1) * slope_keep[h]
        dk_ref[:, head(2 + h)] = dk_lin.astype(BF16)
        dv_lin = dot(key_part[h, 0], dstate[h], 1, 0) + dot(key_part[h, 1], dstate[h], 1, 0)
        dv_ref[:, head(2 + h)] = dv_lin.astype(BF16)

    for step in steps:
        to_dp, flip, cross = step
        index = fin_base + flip * 8 + to_dp * 2 + cross
        pltpu.make_async_remote_copy(
            src_ref=wg_sum.at[0, 0],
            dst_ref=wg_fin.at[0, 0, 0],
            send_sem=ssem.at[index],
            recv_sem=rsem.at[index],
            device_id=column_peer(step),
            device_id_type=MESH,
        ).wait_recv()
    for c in range(2):
        for half in range(2):
            shares = [wg_fin[i, c, half].astype(F32) for i in range(N_DP)]
            total = (shares[0] + shares[1]) + (shares[2] + shares[3])
            first = c * 512 + half * 256
            wg_ref[:, first : first + 256] = total * (1.0 / math.sqrt(N_DP * N_SEQ * ROWS))
    wg_soft.finish()
    wg_lin.finish()
    for copy in started:
        copy.wait_send()
    assert used[0] == N_COPIES, used[0]


N_COPIES = (
    2 * (15 + 7 + 15)
    + 15 + 7 + 8 + 15 + 7 + 1
    + 4 + 1 + 2
    + 2 * (7 + 7)
    + 2
)


def writer(dq, dk, dv, wg, dq_out, dk_out, dv_out, wg_out, sem):
    copies = [
        pltpu.make_async_copy(src, dst, sem.at[i])
        for i, (src, dst) in enumerate(((dq, dq_out), (dk, dk_out), (dv, dv_out), (wg, wg_out)))
    ]
    for copy in copies:
        copy.start()
    for copy in copies:
        copy.wait()


RESULTS = (((ROWS, 512), BF16), ((ROWS, 512), BF16), ((ROWS, 512), BF16), ((4, 1024), F32))


def body(queries, key_rows, value_rows, out_grad, out_weight, norm_gain):
    vmem = pl.BlockSpec(memory_space=pltpu.VMEM)
    hbm = pl.BlockSpec(memory_space=pltpu.HBM)
    out = pl.pallas_call(
        kernel,
        out_shape=tuple(pltpu.VMEM(*result) for result in RESULTS),
        in_specs=[hbm] * 6,
        out_specs=(vmem,) * 4,
        scratch_shapes=[
            pltpu.VMEM((ROWS, 512), BF16),
            pltpu.VMEM((ROWS, 512), BF16),
            pltpu.VMEM((ROWS, 512), BF16),
            pltpu.VMEM((ROWS, 1024), BF16),
            pltpu.VMEM((4, 1024), BF16),
            pltpu.VMEM((2, DH), F32),
            pltpu.VMEM((2, ROWS, SOFT), BF16),
            pltpu.VMEM((2, ROWS, SOFT), BF16),
            pltpu.VMEM((2, 2, ROWS, DH), BF16),
            pltpu.VMEM((2, DH, ROWS), BF16),
            pltpu.VMEM((2, 2, ROWS, DH), BF16),
            pltpu.VMEM((2, ROWS, DH), F32),
            pltpu.VMEM((2, 2, 8, 16, DH), BF16),
            pltpu.VMEM((2, 8, 2, 16, DH), BF16),
            pltpu.VMEM((2, 8, 16, DH), BF16),
            pltpu.VMEM((2, 2, 8, 16, DH), BF16),
            pltpu.VMEM((16, 4, WIDE), BF16),
            pltpu.VMEM((64, WIDE), F32),
            pltpu.VMEM((2, 512, WIDE), BF16),
            pltpu.VMEM((16, 4, 128), BF16),
            pltpu.VMEM((64, 128), F32),
            pltpu.VMEM((2, 8, 64, 128), BF16),
            pltpu.VMEM((2, 512, 128), BF16),
            pltpu.VMEM((ROWS, 512), BF16),
            pltpu.VMEM((ROWS, 512), BF16),
            pltpu.VMEM((ROWS, 512), BF16),
            pltpu.VMEM((2, 3, ROWS, ROWS), F32),
            pltpu.VMEM((2, ROWS, DH), F32),
            pltpu.VMEM((2, 8, 64, 256), BF16),
            pltpu.VMEM((2, 8, 64, 256), BF16),
            pltpu.VMEM((2, 8, 8, 256), BF16),
            pltpu.VMEM((2, 8, 8, 256), BF16),
            pltpu.VMEM((2, 2, 4, 256), BF16),
            pltpu.VMEM((N_DP, 2, 2, 4, 256), BF16),
            pltpu.VMEM((2, 2, ROWS, SOFT), BF16),
            pltpu.VMEM((2, 2, ROWS, SOFT), BF16),
            pltpu.VMEM((2, ROWS, SOFT), F32),
            pltpu.SemaphoreType.DMA((8,)),
            pltpu.SemaphoreType.DMA((N_COPIES + 16,)),
            pltpu.SemaphoreType.DMA((N_COPIES + 16,)),
        ],
        compiler_params=pltpu.CompilerParams(collective_id=0, has_side_effects=True),
        name="sublayer_backward",
    )(
        queries[0],
        key_rows[0],
        value_rows[0],
        out_grad[0],
        out_weight,
        norm_gain.reshape(2, DH),
    )
    out = pl.pallas_call(
        writer,
        out_shape=tuple(jax.ShapeDtypeStruct(*result) for result in RESULTS),
        in_specs=[vmem] * 4,
        out_specs=(hbm,) * 4,
        scratch_shapes=[pltpu.SemaphoreType.DMA((4,))],
        name="write_out",
    )(*[pltpu.with_memory_space_constraint(x, pltpu.VMEM) for x in out])
    return (out[0][None], out[1][None], out[2][None], out[3])


def solution(mesh):
    return jax.shard_map(
        body,
        mesh=mesh,
        in_specs=(
            P("dp", "seq", None),
            P("dp", "seq", None),
            P("dp", "seq", None),
            P("dp", "seq", None),
            P("seq", None),
            P(),
        ),
        out_specs=(
            P("dp", "seq", None),
            P("dp", "seq", None),
            P("dp", "seq", None),
            P("seq", None),
        ),
        check_vma=False,
    )
```

```python
import math

import jax
import jax.numpy as jnp
from jax import lax
from jax.experimental import pallas as pl
from jax.experimental.pallas import tpu as pltpu
from jax.sharding import PartitionSpec as P

MESH = pl.DeviceIdType.MESH
DH = 128
ROWS = 128
SOFT = 256
N_SEQ = 128
N_DP = 4
WIDE = 384
norm_eps = 1e-06
BF16 = jnp.bfloat16
F32 = jnp.float32
FAR = (4, 3, 5, 2, 6, 1, 7)


def dot(a, b, a_dim, b_dim):
    return lax.dot_general(a, b, (((a_dim,), (b_dim,)), ((), ())), preferred_element_type=F32)


def parts(x):
    high = x.astype(BF16)
    return high, (x - high.astype(F32)).astype(BF16)


def dot_wide(a, b, a_dim, b_dim):
    if b.dtype == BF16:
        high, low = parts(a)
        return dot(high, b, a_dim, b_dim) + dot(low, b, a_dim, b_dim)
    if a.dtype == BF16:
        high, low = parts(b)
        return dot(a, high, a_dim, b_dim) + dot(a, low, a_dim, b_dim)
    a_high, a_low = parts(a)
    b_high, b_low = parts(b)
    return (
        dot(a_high, b_high, a_dim, b_dim)
        + dot(a_high, b_low, a_dim, b_dim)
        + dot(a_low, b_high, a_dim, b_dim)
    )


def unit_plus(x):
    return jnp.where(x > 0, x + 1.0, jnp.exp(jnp.minimum(x, 0.0)))


def unit_slope(x):
    return jnp.where(x > 0, 1.0, jnp.exp(jnp.minimum(x, 0.0)))


def head(h):
    return slice(h * DH, (h + 1) * DH)


def kernel(
    q_hbm, k_hbm, v_hbm, g_hbm, w_hbm, gain_hbm,
    dq_ref, dk_ref, dv_ref, wg_ref,
    q_ref, k_ref, v_ref, g_ref, w_ref, gain_ref,
    kx, vx, phi_part, phi_turned, key_part, slope_keep, term, s_xy, s_z, s_full,
    w_in, w_rows, w_all, t_in, t_rows, t_all, t_sorted, g_in, attn_own, attn_in,
    probs, u_keep, wg_out, wg_in, wg_zout, wg_zin, wg_sum, wg_fin,
    back_out, back_in, dkv_keep,
    lsem, ssem, rsem,
):
    dp = lax.axis_index("dp")
    seq = lax.axis_index("seq")
    core = seq % 2
    z = (seq // 2) % 8
    p = seq // 16
    y = p // 4
    other = 1 - core
    partner = seq + 1 - 2 * core
    after = (seq + 1) % N_SEQ
    before = (seq + N_SEQ - 1) % N_SEQ
    factor = DH ** (-0.5)

    loads = [
        pltpu.make_async_copy(src, dst, lsem.at[i])
        for i, (src, dst) in enumerate(
            (
                (k_hbm.at[:, pl.ds(SOFT, SOFT)], k_ref.at[:, pl.ds(SOFT, SOFT)]),
                (v_hbm.at[:, pl.ds(SOFT, SOFT)], v_ref.at[:, pl.ds(SOFT, SOFT)]),
                (w_hbm, w_ref),
                (k_hbm.at[:, pl.ds(0, SOFT)], k_ref.at[:, pl.ds(0, SOFT)]),
                (v_hbm.at[:, pl.ds(0, SOFT)], v_ref.at[:, pl.ds(0, SOFT)]),
                (q_hbm, q_ref),
                (gain_hbm, gain_ref),
                (g_hbm, g_ref),
            )
        )
    ]
    for load in loads:
        load.start()

    def xy_peer(d):
        return (((p + d) % 8) * 8 + z) * 2 + core

    def flat_peer(d, cross):
        return (((p + d) % 8) * 8 + z) * 2 + (core + cross) % 2

    def z_peer(d):
        return (p * 8 + (z + d) % 8) * 2 + core

    def z_cross(d):
        return (p * 8 + (z + d) % 8) * 2 + other

    def column_peer(step):
        to_dp, flip, cross = step
        chip = ((p + 4 * flip) % 8) * 8 + z
        return (dp + to_dp) % N_DP, chip * 2 + (core + cross) % 2

    steps = [(a, b, c) for a in (2, 1, 3, 0) for b in range(2) for c in range(2)][:-4]
    steps += [(0, 1, 1), (0, 1, 0), (0, 0, 1)]

    barrier = pltpu.get_barrier_semaphore()
    peers = [column_peer(step) for step in steps]
    peers += [(dp, z_peer(d)) for d in FAR]
    peers += [(dp, z_cross(d)) for d in FAR]
    peers += [(dp, flat_peer(d, cross)) for d in FAR if d != 4 for cross in range(2)]
    peers += [(dp, after), (dp, before)]
    for peer in peers:
        pl.semaphore_signal(barrier, inc=1, device_id=peer, device_id_type=MESH)

    used = [0]
    started = []
    fin_base = N_COPIES

    def send(src, dst, device, dp_to=None):
        index = used[0]
        used[0] += 1
        copy = pltpu.make_async_remote_copy(
            src_ref=src,
            dst_ref=dst,
            send_sem=ssem.at[index],
            recv_sem=rsem.at[index],
            device_id=(dp if dp_to is None else dp_to, device),
            device_id_type=MESH,
        )
        copy.start()
        started.append(copy)
        return copy

    def arrived(copies):
        for copy in copies:
            copy.wait_recv()

    near = [(d, cross) for d in FAR for cross in range(2)] + [(0, 1)]

    class Total:
        def __init__(self, slot, terms):
            self.i = slot
            for h in range(2):
                term[slot, h] = terms[h].astype(BF16).reshape(8, 16, DH)

        def start(self):
            i = self.i
            self.c = [
                send(term.at[i, (core + cross) % 2, (p + d) % 8], s_xy.at[i, d, cross], flat_peer(d, cross))
                for d, cross in near
            ]

        def along_z(self):
            i = self.i
            arrived(self.c)
            total = term[i, core, p].astype(F32)
            for d, cross in near[::-1]:
                total = total + s_xy[i, d, cross].astype(F32)
            s_z[i, z] = total.astype(BF16)
            self.c = [send(s_z.at[i, z], s_z.at[i, z], z_peer(d)) for d in FAR]

        def spread(self):
            i = self.i
            arrived(self.c)
            total = s_z[i, 0].astype(F32)
            for d in range(1, 8):
                total = total + s_z[i, d].astype(F32)
            s_full[i, core, p] = total.astype(BF16)
            mine = s_full.at[i, core, p]
            self.c = [send(mine, mine, flat_peer(d, cross)) for d, cross in near]

        def value(self):
            arrived(self.c)
            return [s_full[self.i, h].reshape(DH, DH) for h in range(2)]

    class Half:
        def __init__(self, half, g_mine):
            self.s = s = half
            self.own = [dot(attn_own[:, self.rows(b)], g_mine, 0, 0) for b in range(4)]

        def rows(self, b):
            return slice(self.s * SOFT + b * 64, self.s * SOFT + (b + 1) * 64)

        def join(self, g_other):
            s = self.s
            for b in range(4):
                block = (self.own[b] + dot(attn_in[:, self.rows(b)], g_other, 0, 0)).astype(BF16)
                wg_out[s, b] = block[:, 0:256]
                wg_out[s, 4 + b] = block[:, 256:512]

        def xy(self):
            s = self.s
            self.c = [send(wg_out.at[s, (p + d) % 8], wg_in.at[s, d], xy_peer(d)) for d in FAR]

        def along_z(self):
            s = self.s
            arrived(self.c)
            total = wg_out[s, p].astype(F32)
            for d in range(1, 8):
                total = total + wg_in[s, d].astype(F32)
            wg_zout[s] = total.reshape(8, 8, 256).astype(BF16)
            self.c = [send(wg_zout.at[s, (z + d) % 8], wg_zin.at[s, d], z_peer(d)) for d in FAR]

        def deliver(self):
            s = self.s
            arrived(self.c)
            total = wg_zout[s, z].astype(F32)
            for d in range(1, 8):
                total = total + wg_zin[s, d].astype(F32)
            for c in range(2):
                wg_sum[s, c] = total[4 * c : 4 * c + 4]
            flip = (s + y) % 2
            owner = ((s * 4 + p % 4) * 8 + z) * 2

            def copy_to(to_dp, cross):
                index = fin_base + flip * 8 + to_dp * 2 + cross
                core_to = (core + cross) % 2
                return pltpu.make_async_remote_copy(
                    src_ref=wg_sum.at[s, core_to],
                    dst_ref=wg_fin.at[dp, core, y],
                    send_sem=ssem.at[index],
                    recv_sem=rsem.at[index],
                    device_id=((dp + to_dp) % N_DP, owner + core_to),
                    device_id_type=MESH,
                )

            self.out = [copy_to(a, c) for a in (2, 1, 3) for c in range(2)] + [copy_to(0, 1)]
            for copy in self.out:
                copy.start()
            self.last = copy_to(0, 0)

            @pl.when(flip == 1)
            def _():
                self.last.start()

            @pl.when(flip == 0)
            def _():
                wg_fin[dp, core, y] = wg_sum[s, core]

        def finish(self):
            for copy in self.out:
                copy.wait_send()

            @pl.when((self.s + y) % 2 == 1)
            def _():
                self.last.wait_send()

    loads[0].wait()
    loads[1].wait()
    state_sum = Total(
        0,
        [
            dot(unit_plus(k_ref[:, head(2 + h)].astype(F32)).astype(BF16), v_ref[:, head(2 + h)], 0, 0)
            for h in range(2)
        ],
    )
    loads[2].wait()
    w_piece = jnp.where(core == 0, w_ref[:, 0:512].astype(F32), w_ref[:, 512:1024].astype(F32)).astype(BF16)
    w_in[z * 2 + core] = w_piece[:, 0:WIDE]
    t_in[p * 2 + core] = w_piece[:, WIDE:512]

    pl.semaphore_wait(barrier, len(peers))

    state_sum.start()
    def w_part(of, first, width):
        return w_hbm.at[:, pl.ds(pl.multiple_of(of * 512 + first, 128), width)]

    w_slot = w_in.at[z * 2 + core]
    w_copy = [send(w_part(other, 0, WIDE), w_slot, partner)]
    for d in FAR:
        w_copy.append(send(w_part(core, 0, WIDE), w_slot, z_peer(d)))
        w_copy.append(send(w_part(other, 0, WIDE), w_slot, z_cross(d)))
    t_slot = t_in.at[p * 2 + core]
    t_copy = [send(w_part((core + cross) % 2, WIDE, 128), t_slot, flat_peer(d, cross)) for d, cross in near]
    soft = pl.ds(0, SOFT)
    k_copy = [
        send(k_hbm.at[:, soft], kx.at[0], after),
        send(k_hbm.at[:, soft], kx.at[1], before),
    ]
    v_copy = [
        send(v_hbm.at[:, soft], vx.at[0], after),
        send(v_hbm.at[:, soft], vx.at[1], before),
    ]
    g_copy = [
        send(g_hbm.at[:, pl.ds(pl.multiple_of(other * 512, 512), 512)], g_in, partner)
    ]
    for load in loads[3:]:
        load.wait()

    for h in range(2):
        for i, part in enumerate(parts(unit_plus(q_ref[:, head(2 + h)].astype(F32)))):
            phi_part[h, i] = part
            if i == 0:
                phi_turned[h] = part.T
        k_l = k_ref[:, head(2 + h)].astype(F32)
        slope_keep[h] = unit_slope(k_l)
        for i, part in enumerate(parts(unit_plus(k_l))):
            key_part[h, i] = part

    state_sum.along_z()

    arrived(t_copy)
    for i in range(16):
        t_rows[4 * i : 4 * i + 4, :] = t_in[i].astype(F32)
    t_all[core, z] = t_rows[...].astype(BF16)
    t_mine = t_all.at[core, z]
    t_copy = [send(t_mine, t_mine, z_peer(d)) for d in FAR]

    arrived(w_copy)
    for i in range(16):
        w_rows[4 * i : 4 * i + 4, :] = w_in[i].astype(F32)

    def w_block(source):
        return w_all.at[core, pl.ds(pl.multiple_of(source * 64, 64), 64), :]

    w_all[core, pl.ds(pl.multiple_of(p * 64, 64), 64), :] = w_rows[...].astype(BF16)
    w_copy = {d: send(w_block(p), w_block(p), xy_peer(d)) for d in FAR}
    w_swap = [send(w_block(p), w_block(p), partner)]

    row_pos = lax.broadcasted_iota(jnp.int32, (ROWS, ROWS), 0)
    col_pos = lax.broadcasted_iota(jnp.int32, (ROWS, ROWS), 1)
    keep = (col_pos >= row_pos, None, col_pos < row_pos)
    arrived(k_copy)

    def span_of(halo, ref, h):
        return (halo[0, :, head(h)], ref[:, head(h)], halo[1, :, head(h)])

    for h in range(2):
        k_span = span_of(kx, k_ref, h)
        q_h = q_ref[:, head(h)]
        scores = []
        for b in range(3):
            s = dot(q_h, k_span[b], 1, 1) * factor
            scores.append(s if keep[b] is None else jnp.where(keep[b], s, -1e30))
        peak = jnp.max(jnp.maximum(jnp.maximum(scores[0], scores[1]), scores[2]), axis=1, keepdims=True)
        terms = []
        for b in range(3):
            e = jnp.exp(scores[b] - peak)
            terms.append(e if keep[b] is None else jnp.where(keep[b], e, 0.0))
        whole = jnp.sum(terms[0] + terms[1] + terms[2], axis=1, keepdims=True)
        for b in range(3):
            probs[h, b] = terms[b] / whole

    arrived(v_copy)
    for h in range(2):
        v_span = span_of(vx, v_ref, h)
        total = dot(probs[h, 0].astype(BF16), v_span[0], 1, 0)
        for b in range(1, 3):
            total = total + dot(probs[h, b].astype(BF16), v_span[b], 1, 0)
        attn_own[:, head(h)] = total.astype(BF16)
    a_copy = [send(attn_own.at[:, soft], attn_in.at[:, soft], partner)]

    state_sum.spread()

    g_mine = g_ref[:, pl.ds(pl.multiple_of(core * 512, 512), 512)]
    wg_soft = Half(0, g_mine)
    arrived(g_copy)
    arrived(a_copy)
    wg_soft.join(g_in[...])
    wg_soft.xy()

    for d in FAR[::-1]:
        w_copy[d].wait_recv()
        block = w_block((p + 8 - d) % 8)
        w_swap.append(send(block, block, partner))
    arrived(t_copy)
    w_swap.append(send(t_all.at[core], t_all.at[core], partner))

    def t_sort(c, groups):
        for group in groups:
            for i in range(8):
                first = group * 64 + i * 8
                t_sorted[c, first : first + 8, :] = t_all[c, i, group * 8 : group * 8 + 8, :]

    def d_attn_of(c, rows):
        g_wide = g_ref[:, pl.ds(pl.multiple_of(c * 512, 128), WIDE)]
        g_rest = g_ref[:, pl.ds(pl.multiple_of(c * 512 + WIDE, 128), 128)]
        return dot(g_wide, w_all[c, rows, :], 1, 1) + dot(g_rest, t_sorted[c, rows, :], 1, 1)

    t_sort(core, range(4, 8))
    mine_lin = d_attn_of(core, slice(SOFT, 512))

    state = state_sum.value()

    lin_r = []
    for h in range(2):
        u = dot(phi_part[h, 0], state[h], 1, 0) + dot(phi_part[h, 1], state[h], 1, 0)
        r = lax.rsqrt(jnp.mean(u * u, axis=1, keepdims=True) + norm_eps)
        u_keep[h] = u
        lin_r.append(r)
        attn_own[:, head(2 + h)] = (gain_ref[h : h + 1, :] * u * r).astype(BF16)
    lin = pl.ds(SOFT, SOFT)
    a_copy = [send(attn_own.at[:, lin], attn_in.at[:, lin], partner)]

    wg_lin = Half(1, g_mine)
    arrived(a_copy)
    wg_lin.join(g_in[...])
    arrived(w_swap)
    t_sort(other, range(4, 8))
    d_attn_lin = (mine_lin + d_attn_of(other, slice(SOFT, 512))).astype(BF16)

    grad_u = []
    for h in range(2):
        g_lin = gain_ref[h : h + 1, :] * d_attn_lin[:, head(h)].astype(F32)
        u = u_keep[h]
        r = lin_r[h]
        grad_u.append(r * g_lin - u * (r * r * r) * jnp.mean(g_lin * u, axis=1, keepdims=True))
    terms = []
    for h in range(2):
        terms.append(dot(phi_turned[h], grad_u[h].astype(BF16), 1, 0))
    grad_sum = Total(1, terms)
    grad_sum.start()
    wg_lin.xy()

    for c in range(2):
        t_sort(c, range(4))
    d_attn = (d_attn_of(0, slice(0, SOFT)) + d_attn_of(1, slice(0, SOFT))).astype(BF16)
    wg_soft.along_z()

    for h in range(2):
        k_span = span_of(kx, k_ref, h)
        v_span = span_of(vx, v_ref, h)
        q_h = q_ref[:, head(h)]
        da = d_attn[:, head(h)]
        delta = jnp.sum(da.astype(F32) * attn_own[:, head(h)].astype(F32), axis=1, keepdims=True)
        dq = None
        for b in range(3):
            pr = probs[h, b]
            ds = (pr * (dot(da, v_span[b], 1, 1) - delta)).astype(BF16)
            step = dot(ds, k_span[b], 1, 0)
            dq = step if dq is None else dq + step
            dk = dot(ds, q_h, 0, 0) * factor
            dv = dot(pr.astype(BF16), da, 0, 0)
            if b == 1:
                dkv_keep[0, :, head(h)] = dk
                dkv_keep[1, :, head(h)] = dv
            else:
                back_out[b // 2, 0, :, head(h)] = dk.astype(BF16)
                back_out[b // 2, 1, :, head(h)] = dv.astype(BF16)
        dq_ref[:, head(h)] = (dq * factor).astype(BF16)
    grad_sum.along_z()

    back_copy = [
        send(back_out.at[0], back_in.at[0], before),
        send(back_out.at[1], back_in.at[1], after),
    ]

    for h in range(2):
        q_lin = q_ref[:, head(2 + h)].astype(F32)
        dq_lin = dot_wide(grad_u[h], state[h], 1, 1) * unit_slope(q_lin)
        dq_ref[:, head(2 + h)] = dq_lin.astype(BF16)

    wg_lin.along_z()
    wg_soft.deliver()
    grad_sum.spread()

    arrived(back_copy)
    for h in range(2):
        for t, out in ((0, dk_ref), (1, dv_ref)):
            total = dkv_keep[t, :, head(h)] + back_in[1, t, :, head(h)].astype(F32)
            total = total + back_in[0, t, :, head(h)].astype(F32)
            out[:, head(h)] = total.astype(BF16)

    wg_lin.deliver()
    dstate = grad_sum.value()
    for h in range(2):
        dk_lin = dot(v_ref[:, head(2 + h)], dstate[h], 1, 1) * slope_keep[h]
        dk_ref[:, head(2 + h)] = dk_lin.astype(BF16)
        dv_lin = dot(key_part[h, 0], dstate[h], 1, 0) + dot(key_part[h, 1], dstate[h], 1, 0)
        dv_ref[:, head(2 + h)] = dv_lin.astype(BF16)

    for step in steps:
        to_dp, flip, cross = step
        index = fin_base + flip * 8 + to_dp * 2 + cross
        pltpu.make_async_remote_copy(
            src_ref=wg_sum.at[0, 0],
            dst_ref=wg_fin.at[0, 0, 0],
            send_sem=ssem.at[index],
            recv_sem=rsem.at[index],
            device_id=column_peer(step),
            device_id_type=MESH,
        ).wait_recv()
    for c in range(2):
        for half in range(2):
            total = (wg_fin[0, c, half] + wg_fin[1, c, half]) + (wg_fin[2, c, half] + wg_fin[3, c, half])
            first = c * 512 + half * 256
            wg_ref[:, first : first + 256] = total * (1.0 / math.sqrt(N_DP * N_SEQ * ROWS))
    wg_soft.finish()
    wg_lin.finish()
    for copy in started:
        copy.wait_send()
    assert used[0] == N_COPIES, used[0]


N_COPIES = (
    2 * (15 + 7 + 15)
    + 15 + 7 + 8 + 15 + 7 + 1
    + 4 + 1 + 2
    + 2 * (7 + 7)
    + 2
)


def writer(dq, dk, dv, wg, dq_out, dk_out, dv_out, wg_out, sem):
    copies = [
        pltpu.make_async_copy(src, dst, sem.at[i])
        for i, (src, dst) in enumerate(((dq, dq_out), (dk, dk_out), (dv, dv_out), (wg, wg_out)))
    ]
    for copy in copies:
        copy.start()
    for copy in copies:
        copy.wait()


RESULTS = (((ROWS, 512), BF16), ((ROWS, 512), BF16), ((ROWS, 512), BF16), ((4, 1024), F32))


def body(queries, key_rows, value_rows, out_grad, out_weight, norm_gain):
    vmem = pl.BlockSpec(memory_space=pltpu.VMEM)
    hbm = pl.BlockSpec(memory_space=pltpu.HBM)
    out = pl.pallas_call(
        kernel,
        out_shape=tuple(pltpu.VMEM(*result) for result in RESULTS),
        in_specs=[hbm] * 6,
        out_specs=(vmem,) * 4,
        scratch_shapes=[
            pltpu.VMEM((ROWS, 512), BF16),
            pltpu.VMEM((ROWS, 512), BF16),
            pltpu.VMEM((ROWS, 512), BF16),
            pltpu.VMEM((ROWS, 1024), BF16),
            pltpu.VMEM((4, 1024), BF16),
            pltpu.VMEM((2, DH), F32),
            pltpu.VMEM((2, ROWS, SOFT), BF16),
            pltpu.VMEM((2, ROWS, SOFT), BF16),
            pltpu.VMEM((2, 2, ROWS, DH), BF16),
            pltpu.VMEM((2, DH, ROWS), BF16),
            pltpu.VMEM((2, 2, ROWS, DH), BF16),
            pltpu.VMEM((2, ROWS, DH), F32),
            pltpu.VMEM((2, 2, 8, 16, DH), BF16),
            pltpu.VMEM((2, 8, 2, 16, DH), BF16),
            pltpu.VMEM((2, 8, 16, DH), BF16),
            pltpu.VMEM((2, 2, 8, 16, DH), BF16),
            pltpu.VMEM((16, 4, WIDE), BF16),
            pltpu.VMEM((64, WIDE), F32),
            pltpu.VMEM((2, 512, WIDE), BF16),
            pltpu.VMEM((16, 4, 128), BF16),
            pltpu.VMEM((64, 128), F32),
            pltpu.VMEM((2, 8, 64, 128), BF16),
            pltpu.VMEM((2, 512, 128), BF16),
            pltpu.VMEM((ROWS, 512), BF16),
            pltpu.VMEM((ROWS, 512), BF16),
            pltpu.VMEM((ROWS, 512), BF16),
            pltpu.VMEM((2, 3, ROWS, ROWS), F32),
            pltpu.VMEM((2, ROWS, DH), F32),
            pltpu.VMEM((2, 8, 64, 256), BF16),
            pltpu.VMEM((2, 8, 64, 256), BF16),
            pltpu.VMEM((2, 8, 8, 256), BF16),
            pltpu.VMEM((2, 8, 8, 256), BF16),
            pltpu.VMEM((2, 2, 4, 256), F32),
            pltpu.VMEM((N_DP, 2, 2, 4, 256), F32),
            pltpu.VMEM((2, 2, ROWS, SOFT), BF16),
            pltpu.VMEM((2, 2, ROWS, SOFT), BF16),
            pltpu.VMEM((2, ROWS, SOFT), F32),
            pltpu.SemaphoreType.DMA((8,)),
            pltpu.SemaphoreType.DMA((N_COPIES + 16,)),
            pltpu.SemaphoreType.DMA((N_COPIES + 16,)),
        ],
        compiler_params=pltpu.CompilerParams(collective_id=0, has_side_effects=True),
        name="sublayer_backward",
    )(
        queries[0],
        key_rows[0],
        value_rows[0],
        out_grad[0],
        out_weight,
        norm_gain.reshape(2, DH),
    )
    out = pl.pallas_call(
        writer,
        out_shape=tuple(jax.ShapeDtypeStruct(*result) for result in RESULTS),
        in_specs=[vmem] * 4,
        out_specs=(hbm,) * 4,
        scratch_shapes=[pltpu.SemaphoreType.DMA((4,))],
        name="write_out",
    )(*[pltpu.with_memory_space_constraint(x, pltpu.VMEM) for x in out])
    return (out[0][None], out[1][None], out[2][None], out[3])


def solution(mesh):
    return jax.shard_map(
        body,
        mesh=mesh,
        in_specs=(
            P("dp", "seq", None),
            P("dp", "seq", None),
            P("dp", "seq", None),
            P("dp", "seq", None),
            P("seq", None),
            P(),
        ),
        out_specs=(
            P("dp", "seq", None),
            P("dp", "seq", None),
            P("dp", "seq", None),
            P("seq", None),
        ),
        check_vma=False,
    )
```
